32 devices in a mesh: wide: 16 (over z, x, core), narrow: 2 (over y).
Axes of the slice: x: 2, y: 2, z: 4, core: 2. Of those that a mesh axis runs over, the one named last changes fastest.
Arguments:
- latents: bfloat16 [65536, 1024], P(('wide', 'narrow')), may hold values from -6 to 6
- cotangent: bfloat16 [65536, 1024], P(('wide', 'narrow')), may hold values from -6 to 6
- crop_counts: int32 [16], replicated, may hold values from 1 to 8, as said below
- image_device: int32 [16], replicated, may hold values from 0 to 15, as said below
- query_weight: bfloat16 [1024, 1024], P(None, 'narrow'), may hold values from -0.1875 to 0.1875
- key_weight: bfloat16 [1024, 1024], P(None, 'narrow'), may hold values from -0.1875 to 0.1875
- value_weight: bfloat16 [1024, 1024], P(None, 'narrow'), may hold values from -0.1875 to 0.1875
- out_weight: bfloat16 [1024, 1024], P('narrow'), may hold values from -2 to 2
- up_weight: bfloat16 [1024, 1024], P(None, 'narrow'), may hold values from -0.1875 to 0.1875
- down_weight: bfloat16 [1024, 1024], P('narrow'), may hold values from -0.1875 to 0.1875
- query_bias: bfloat16 [1024], P('narrow'), may hold values from -3 to 3
- value_bias: bfloat16 [1024], P('narrow'), may hold values from -3 to 3
- up_bias: bfloat16 [1024], P('narrow'), may hold values from -3 to 3
- out_bias: float32 [1024], replicated, may hold values from -2 to 2
- down_bias: float32 [1024], replicated, may hold values from -2 to 2
- first_gain: float32 [1024], replicated, may hold values from 0.5 to 1.5
- first_shift: float32 [1024], replicated, may hold values from -1.2 to 1.2
- second_gain: float32 [1024], replicated, may hold values from 0.5 to 1.5
- second_shift: float32 [1024], replicated, may hold values from -1.2 to 1.2
Outputs:
- block_output: bfloat16 [65536, 1024], P(('wide', 'narrow'))
- latents_gradient: float32 [65536, 1024], P(('wide', 'narrow'))
- query_weight_gradient: float32 [1024, 1024], P(None, 'narrow')
- key_weight_gradient: float32 [1024, 1024], P(None, 'narrow')
- value_weight_gradient: float32 [1024, 1024], P(None, 'narrow')
- out_weight_gradient: float32 [1024, 1024], P('narrow')
- up_weight_gradient: float32 [1024, 1024], P(None, 'narrow')
- down_weight_gradient: float32 [1024, 1024], P('narrow')
- query_bias_gradient: float32 [1024], P('narrow')
- value_bias_gradient: float32 [1024], P('narrow')
- up_bias_gradient: float32 [1024], P('narrow')
- out_bias_gradient: float32 [1024], replicated
- down_bias_gradient: float32 [1024], replicated
- first_gain_gradient: float32 [1024], replicated
- first_shift_gradient: float32 [1024], replicated
- second_gain_gradient: float32 [1024], replicated
- second_shift_gradient: float32 [1024], replicated
The draws below stay inside these ranges and needn't reach their ends.
Inputs may be any that keep to these rules, and one draw needn't show every extreme that they name: `crop_counts`: each image holds 1 to 8 crops; the images of one wide index hold 8 crops or fewer together, and some wide index holds exactly 8. `image_device`: every wide index receives exactly one image.
All inputs are finite; a program needn't handle non-finite values.
Results may differ from the reference program's by a relative error of at most 0.02.
Values may be sent and summed in bfloat16 or wider, within the bound.
No kernel may reach another device: no remote copies, remote signals or barrier semaphores. Data moves between devices by JAX's collectives and lax.ppermute only.
A program may use at most 192 MiB of HBM per device.

```python
import math
import jax
import jax.numpy as jnp
from jax import lax

D = 1024
H = 8
HS = 128
F = 1024
CROP = 512
MAXC = 8
IMAGES = 16
CAP = 8
GROUP = 4096
ROWS = 65536
N_WIDE = 16


def image_plan(key):
    order = jax.random.permutation(jax.random.fold_in(key, 11), IMAGES)
    owner = (order % N_WIDE).astype(jnp.int32)
    counts = jax.random.randint(jax.random.fold_in(key, 12), (IMAGES,), 1, MAXC + 1, dtype=jnp.int32)
    full_owner = jax.random.randint(jax.random.fold_in(key, 13), (), 0, N_WIDE, dtype=jnp.int32)
    light_owner = (full_owner + 1) % N_WIDE
    counts = jnp.where(owner == full_owner, MAXC, counts)
    counts = jnp.where(owner == light_owner, 1, counts)
    return (counts.astype(jnp.int32), owner)


def draw_crop_counts(key, part):
    return image_plan(key)[0]


def draw_image_device(key, part):
    return image_plan(key)[1]


def level_of(own_key, shape, cuts, least, high):
    def one(dim, parts):
        draws = jax.random.uniform(jax.random.fold_in(jax.random.fold_in(own_key, 6), dim), (parts,), jnp.float32, least / len(cuts), high / len(cuts))
        return jnp.repeat(jnp.exp(draws), shape[dim] // parts).reshape((-1,) + (1,) * (len(shape) - dim - 1))

    loudness = one(*cuts[0])
    for cut in cuts[1:]:
        loudness = loudness * one(*cut)
    return loudness


def normal_values(key, extent, width, most, cuts=(), kind=jnp.bfloat16):
    level = level_of(key, extent, cuts, -0.22, 0.18) if cuts else 1.0
    values = jax.random.normal(key, extent, jnp.float32) * width * level
    return jnp.minimum(jnp.maximum(values, -most), most).astype(kind)


def setup_inputs(seed: int = 0) -> dict:
    splits = jax.random.split(jax.random.key(seed), 20)
    return {
        "latents": normal_values(splits[0], (ROWS, D), 1.0, 6.0, ((0, 32),)),
        "cotangent": normal_values(splits[1], (ROWS, D), 1.0, 6.0, ((0, 32),)),
        "crop_counts": draw_crop_counts(jax.random.fold_in(splits[19], 71), 0),
        "image_device": draw_image_device(jax.random.fold_in(splits[19], 71), 0),
        "query_weight": normal_values(splits[4], (D, D), D ** -0.5, 0.1875, ((1, 2),)),
        "key_weight": normal_values(splits[5], (D, D), D ** -0.5, 0.1875, ((1, 2),)),
        "value_weight": normal_values(splits[6], (D, D), D ** -0.5, 0.1875, ((1, 2),)),
        "out_weight": normal_values(splits[7], (D, D), (max(D // 128, 1)) ** -0.5, 2.0, ((0, 2),)),
        "up_weight": normal_values(splits[8], (D, F), D ** -0.5, 0.1875, ((1, 2),)),
        "down_weight": normal_values(splits[9], (F, D), F ** -0.5, 0.1875, ((0, 2),)),
        "query_bias": normal_values(splits[10], (D,), 0.5, 3.0, ((0, 2),)),
        "value_bias": normal_values(splits[11], (D,), 0.5, 3.0, ((0, 2),)),
        "up_bias": normal_values(splits[12], (F,), 0.5, 3.0, ((0, 2),)),
        "out_bias": normal_values(splits[13], (D,), 0.3, 2.0, (), jnp.float32),
        "down_bias": normal_values(splits[14], (D,), 0.3, 2.0, (), jnp.float32),
        "first_gain": jnp.clip(1.0 + 0.1 * jax.random.normal(splits[15], (D,), jnp.float32), 0.5, 1.5),
        "first_shift": normal_values(splits[16], (D,), 0.2, 1.2, (), jnp.float32),
        "second_gain": jnp.clip(1.0 + 0.1 * jax.random.normal(splits[17], (D,), jnp.float32), 0.5, 1.5),
        "second_shift": normal_values(splits[18], (D,), 0.2, 1.2, (), jnp.float32),
    }


EPSILON = 1e-05
HIGH = lax.Precision.HIGHEST

@jax.custom_vjp
def low(v):
    return lax.optimization_barrier(v.astype(jnp.bfloat16)).astype(jnp.float32)

@jax.custom_vjp
def low_back(v):
    return v

def low_keep(v):
    return (low(v), None)

def low_pass(kept, grad):
    return (grad,)

def back_keep(v):
    return (v, None)

def back_low(kept, grad):
    return (low(grad),)
low.defvjp(low_keep, low_pass)
low_back.defvjp(back_keep, back_low)

def layer_norm(values, gain, shift):
    center = values - lax.optimization_barrier(jnp.mean(values, axis=-1, keepdims=True))
    variance = lax.optimization_barrier(jnp.mean(center * center, axis=-1, keepdims=True))
    return center * lax.rsqrt(variance + EPSILON) * gain + shift

def matmul(left, right):
    return jnp.dot(left, right, precision=HIGH, preferred_element_type=jnp.float32)

def crop_attention(item):
    query, keys, values = item
    scale = 1.0 / math.sqrt(HS)
    scores = low_back(jnp.einsum('qhd,khd->hqk', query, keys, precision=HIGH) * scale)
    probs = jax.nn.softmax(scores, axis=-1)
    mixed = jnp.einsum('hqk,khd->qhd', low(probs), values, precision=HIGH)
    return low(low_back(mixed))

def block_forward(latent_rows, query_weight, key_weight, value_weight, out_weight, up_weight, down_weight, query_bias, value_bias, up_bias, out_bias, down_bias, first_gain, first_shift, second_gain, second_shift):
    count = latent_rows.shape[0]
    shape = (count // CROP, CROP, H, HS)
    first_normed = low(layer_norm(latent_rows, first_gain, first_shift))
    query = low(low_back(matmul(first_normed, query_weight) + query_bias)).reshape(shape)
    keys = low(low_back(matmul(first_normed, key_weight))).reshape(shape)
    values = low(low_back(matmul(first_normed, value_weight) + value_bias)).reshape(shape)
    attended = lax.map(jax.checkpoint(crop_attention), (query, keys, values)).reshape(count, D)
    hidden = latent_rows + low_back(matmul(attended, out_weight)) + out_bias
    second_normed = low(layer_norm(hidden, second_gain, second_shift))
    before = low_back(matmul(second_normed, up_weight) + up_bias)
    activated = low(jax.nn.gelu(before, approximate=False))
    return hidden + low_back(matmul(activated, down_weight)) + down_bias

def reference(latents, cotangent, crop_counts, image_device, query_weight, key_weight, value_weight, out_weight, up_weight, down_weight, query_bias, value_bias, up_bias, out_bias, down_bias, first_gain, first_shift, second_gain, second_shift):
    owners = image_device[:, None] == jnp.arange(N_WIDE, dtype=jnp.int32)[None, :]
    live_count = lax.optimization_barrier(jnp.sum(jnp.where(owners, crop_counts[:, None], 0), axis=0))
    slots = jnp.arange(CAP, dtype=jnp.int32)
    live = (slots[None, :] < live_count[:, None]).astype(jnp.float32)
    live_rows = jnp.repeat(live, CROP, axis=1)[..., None]
    inputs = latents.astype(jnp.float32).reshape(N_WIDE, GROUP, D)
    upstream = cotangent.astype(jnp.float32).reshape(N_WIDE, GROUP, D) * live_rows
    params = tuple((p.astype(jnp.float32) for p in (query_weight, key_weight, value_weight, out_weight, up_weight, down_weight, query_bias, value_bias, up_bias, out_bias, down_bias, first_gain, first_shift, second_gain, second_shift)))

    def one_group(totals, item):
        group_rows, group_upstream = item
        result, pull = jax.vjp(block_forward, group_rows, *params)
        grads = pull(group_upstream)
        totals = tuple((a + b for a, b in zip(totals, grads[1:])))
        return (totals, (result, grads[0]))
    zeros = tuple((jnp.zeros_like(p) for p in params))
    totals, (results, input_grads) = lax.scan(one_group, zeros, (inputs, upstream))
    block_output = (results * live_rows).reshape(ROWS, D).astype(jnp.bfloat16)
    latents_gradient = input_grads.reshape(ROWS, D)
    return (block_output, latents_gradient, totals[0], totals[1], totals[2], totals[3], totals[4], totals[5], totals[6], totals[7], totals[8], totals[9], totals[10], totals[11], totals[12], totals[13], totals[14])
```

```python
from functools import partial
import math

import jax
import jax.numpy as jnp
from jax import lax
from jax.sharding import PartitionSpec as P

HS = 128
CROP = 512


EPSILON = 1e-05


def normalize(values, gain, shift):
    center = values - jnp.mean(values, axis=-1, keepdims=True)
    inverse = lax.rsqrt(jnp.mean(center * center, axis=-1, keepdims=True) + EPSILON)
    unit = center * inverse
    return (unit * gain + shift, unit, inverse)


def normalize_back(upstream, unit, inverse, gain):
    scaled = upstream * gain
    inner = scaled - jnp.mean(scaled, axis=-1, keepdims=True)
    inner = inner - unit * jnp.mean(scaled * unit, axis=-1, keepdims=True)
    return (inner * inverse, jnp.sum(upstream * unit, axis=0), jnp.sum(upstream, axis=0))


def matmul(left, right):
    return jnp.dot(left, right, preferred_element_type=jnp.float32)


def matmul_left(left, right):
    return lax.dot_general(
        left, right, (((0,), (0,)), ((), ())), preferred_element_type=jnp.float32
    )


def matmul_right(left, right):
    return lax.dot_general(
        left, right, (((1,), (1,)), ((), ())), preferred_element_type=jnp.float32
    )


def heads_of(array):
    count, width = array.shape
    return array.reshape(count // CROP, CROP, width // HS, HS).transpose(0, 2, 1, 3)


def rows_of(array):
    crops, heads, rows, size = array.shape
    return array.transpose(0, 2, 1, 3).reshape(crops * rows, heads * size)


def batched(left, right, left_dim, right_dim):
    return lax.dot_general(
        left,
        right,
        (((left_dim,), (right_dim,)), ((0, 1), (0, 1))),
        preferred_element_type=jnp.float32,
    )


def pair_perm(size, bit):
    return [(i, i ^ bit) for i in range(size)]


class Links:
    def __init__(self):
        self.wide = lax.axis_size("wide")
        self.narrow = lax.axis_size("narrow")
        self.paired = self.narrow == 2 and self.wide == 16
        self.index = lax.axis_index("wide")
        self.core = self.index % 2

    def swap(self, array, bit):
        return lax.ppermute(array, "wide", pair_perm(self.wide, bit))

    def swap_narrow(self, array):
        return lax.ppermute(array, "narrow", [(0, 1), (1, 0)])

    def others(self, weight, axis):
        if not self.paired:
            whole = lax.all_gather(weight, "narrow", axis=0, tiled=False)
            whole = jnp.roll(whole, -lax.axis_index("narrow"), axis=0)[1:]
            return jnp.concatenate([whole[i] for i in range(self.narrow - 1)], axis=axis)
        half = weight.shape[0] // 2
        mine = lax.dynamic_slice_in_dim(weight, self.core * half, half, 0)
        near = self.swap_narrow(mine)
        far = self.swap(near, 1)
        first = jnp.where(self.core == 0, near, far)
        second = jnp.where(self.core == 0, far, near)
        return jnp.concatenate([first, second], axis=0)

    def halves(self, array, bit):
        half = array.shape[0] // 2
        position = (self.index // bit) % 2
        keep = lax.dynamic_slice_in_dim(array, position * half, half, 0)
        give = lax.dynamic_slice_in_dim(array, (1 - position) * half, half, 0)
        return keep, give

    def add(self, left, right):
        return (left.astype(jnp.float32) + right.astype(jnp.float32)).astype(jnp.bfloat16)

    def join(self, mine, other, bit):
        position = (self.index // bit) % 2
        first = jnp.where(position == 0, mine, other)
        second = jnp.where(position == 0, other, mine)
        return jnp.concatenate([first, second], axis=0)

    def reduce_matrix(self, own, other, axis):
        own = own.astype(jnp.bfloat16)
        other = other.astype(jnp.bfloat16)
        if not self.paired:
            width = own.shape[axis]
            parts = jnp.stack(
                [own]
                + [
                    lax.slice_in_dim(other, i * width, (i + 1) * width, axis=axis)
                    for i in range(self.narrow - 1)
                ]
            )
            parts = jnp.roll(parts, lax.axis_index("narrow"), axis=0)
            mine = lax.psum_scatter(parts, "narrow", scatter_dimension=0, tiled=True)[0]
            return lax.psum(mine, "wide").astype(jnp.float32)
        keep_own, give_own = self.halves(own, 1)
        keep_other, give_other = self.halves(other, 1)
        keep_other = self.add(keep_other, self.swap(give_other, 1))
        keep = self.add(keep_own, self.swap(give_own, 1))
        keep = self.add(keep, self.swap_narrow(keep_other))
        for bit in (2, 4, 8):
            keep, give = self.halves(keep, bit)
            keep = self.add(keep, self.swap(give, bit))
        for bit in (8, 4, 2, 1):
            keep = self.join(keep, self.swap(keep, bit), bit)
        return keep.astype(jnp.float32)

    def reduce_all(self, rows):
        if not self.paired:
            return lax.psum(rows, ("wide", "narrow"))
        rows = rows + self.swap(rows, 1)
        rows = rows + self.swap_narrow(rows)
        for bit in (2, 4, 8):
            rows = rows + self.swap(rows, bit)
        return rows


def on_device(
    latents,
    cotangent,
    crop_counts,
    image_device,
    query_weight,
    key_weight,
    value_weight,
    out_weight,
    up_weight,
    down_weight,
    query_bias,
    value_bias,
    up_bias,
    out_bias,
    down_bias,
    first_gain,
    first_shift,
    second_gain,
    second_shift,
):
    links = Links()
    count = latents.shape[0]
    narrow = links.narrow
    owned = jnp.sum(jnp.where(image_device == lax.axis_index("wide"), crop_counts, 0))
    first_row = lax.axis_index("narrow") * count
    crop_index = (first_row + jnp.arange(count, dtype=jnp.int32)) // CROP
    live = (crop_index < owned).astype(jnp.float32)[:, None]
    biases = jnp.stack([query_bias, value_bias, up_bias])
    biases = lax.all_gather(biases, "narrow", axis=0)
    biases = jnp.roll(biases, -lax.axis_index("narrow"), axis=0)
    biases = biases.transpose(1, 0, 2).reshape(3, -1).astype(jnp.float32)
    units = query_weight.shape[1]
    query_full = jnp.concatenate([query_weight, links.others(query_weight, 1)], axis=1)
    key_full = jnp.concatenate([key_weight, links.others(key_weight, 1)], axis=1)
    value_full = jnp.concatenate([value_weight, links.others(value_weight, 1)], axis=1)
    out_full = jnp.concatenate([out_weight, links.others(out_weight, 0)], axis=0)
    up_full = jnp.concatenate([up_weight, links.others(up_weight, 1)], axis=1)
    down_full = jnp.concatenate([down_weight, links.others(down_weight, 0)], axis=0)
    scale = 1.0 / math.sqrt(HS)

    latent_rows = latents.astype(jnp.float32)
    first_normed, first_unit, first_inverse = normalize(latent_rows, first_gain, first_shift)
    first_all = first_normed.astype(jnp.bfloat16)
    query = heads_of((matmul(first_all, query_full) + biases[0]).astype(jnp.bfloat16))
    keys = heads_of(matmul(first_all, key_full).astype(jnp.bfloat16))
    values = heads_of((matmul(first_all, value_full) + biases[1]).astype(jnp.bfloat16))
    scores = batched(query, keys, 3, 3) * scale
    probs = jax.nn.softmax(scores, axis=-1)
    probs_low = probs.astype(jnp.bfloat16)
    attended = rows_of(batched(probs_low, values, 3, 2).astype(jnp.bfloat16))
    hidden = latent_rows + matmul(attended, out_full) + out_bias
    second_normed, second_unit, second_inverse = normalize(hidden, second_gain, second_shift)
    second_all = second_normed.astype(jnp.bfloat16)
    before = matmul(second_all, up_full) + biases[2]
    gelu_value, gelu_pull = jax.vjp(partial(jax.nn.gelu, approximate=False), before)
    activated = gelu_value.astype(jnp.bfloat16)
    result = hidden + matmul(activated, down_full) + down_bias
    block_output = (result * live).astype(jnp.bfloat16)
    top_grad = cotangent.astype(jnp.float32) * live
    down_bias_grad = jnp.sum(top_grad, axis=0)
    top_all = top_grad.astype(jnp.bfloat16)
    down_grad = matmul_left(activated, top_all)
    activated_grad = matmul_right(top_all, down_full)
    before_grad = gelu_pull(activated_grad)[0].astype(jnp.bfloat16)
    upbias_grad = jnp.sum(before_grad.astype(jnp.float32), axis=0)
    up_grad = matmul_left(second_all, before_grad)
    second_grad = matmul_right(before_grad, up_full)
    hidden_part, second_gain_grad, second_shift_grad = normalize_back(
        second_grad, second_unit, second_inverse, second_gain
    )
    hidden_grad = top_grad + hidden_part
    out_bias_grad = jnp.sum(hidden_grad, axis=0)
    hidden_all = hidden_grad.astype(jnp.bfloat16)
    out_grad = matmul_left(attended, hidden_all)
    attended_grad = heads_of(matmul_right(hidden_all, out_full).astype(jnp.bfloat16))
    values_raw = batched(probs_low, attended_grad, 2, 2)
    probs_grad = batched(attended_grad, values, 3, 3)
    inner = jnp.sum(probs * probs_grad, axis=-1, keepdims=True)
    scores_grad = (probs * (probs_grad - inner)).astype(jnp.bfloat16)
    query_grad = rows_of((batched(scores_grad, keys, 3, 2) * scale).astype(jnp.bfloat16))
    keys_grad = rows_of((batched(scores_grad, query, 2, 2) * scale).astype(jnp.bfloat16))
    values_grad = rows_of(values_raw.astype(jnp.bfloat16))
    qbias_grad = jnp.sum(query_grad.astype(jnp.float32), axis=0)
    vbias_grad = jnp.sum(values_grad.astype(jnp.float32), axis=0)
    query_wgrad = matmul_left(first_all, query_grad)
    key_wgrad = matmul_left(first_all, keys_grad)
    value_wgrad = matmul_left(first_all, values_grad)
    part = matmul_right(query_grad, query_full)
    part = part + matmul_right(keys_grad, key_full)
    first_grad = part + matmul_right(values_grad, value_full)
    input_part, first_gain_grad, first_shift_grad = normalize_back(
        first_grad, first_unit, first_inverse, first_gain
    )
    latents_gradient = hidden_grad + input_part

    def shared_units(vector):
        if narrow == 2:
            swapped = jnp.concatenate([vector[units:], vector[:units]])
            return jnp.where(lax.axis_index("narrow") == 0, vector, swapped)
        return jnp.roll(vector.reshape(narrow, units), lax.axis_index("narrow"), axis=0).reshape(-1)

    rows = jnp.stack(
        [
            first_gain_grad,
            first_shift_grad,
            second_gain_grad,
            second_shift_grad,
            out_bias_grad,
            down_bias_grad,
            shared_units(qbias_grad),
            shared_units(vbias_grad),
            shared_units(upbias_grad),
        ]
    )
    rowwise = links.reduce_all(rows)
    own = lax.dynamic_slice_in_dim(rowwise[6:], lax.axis_index("narrow") * units, units, 1)
    matrices = (
        links.reduce_matrix(query_wgrad[:, :units], query_wgrad[:, units:], 1),
        links.reduce_matrix(key_wgrad[:, :units], key_wgrad[:, units:], 1),
        links.reduce_matrix(value_wgrad[:, :units], value_wgrad[:, units:], 1),
        links.reduce_matrix(out_grad[:units], out_grad[units:], 0),
        links.reduce_matrix(up_grad[:, :units], up_grad[:, units:], 1),
        links.reduce_matrix(down_grad[:units], down_grad[units:], 0),
    )
    return (
        block_output,
        latents_gradient,
        *matrices,
        own[0],
        own[1],
        own[2],
        rowwise[4],
        rowwise[5],
        rowwise[0],
        rowwise[1],
        rowwise[2],
        rowwise[3],
    )


def solution(mesh):
    rows = P(("wide", "narrow"), None)
    columns = P(None, "narrow")
    units = P("narrow", None)
    vector = P("narrow")
    whole = P()
    return jax.shard_map(
        on_device,
        mesh=mesh,
        in_specs=(
            rows,
            rows,
            whole,
            whole,
            columns,
            columns,
            columns,
            units,
            columns,
            units,
            vector,
            vector,
            vector,
            whole,
            whole,
            whole,
            whole,
            whole,
            whole,
        ),
        out_specs=(
            rows,
            rows,
            columns,
            columns,
            columns,
            units,
            columns,
            units,
            vector,
            vector,
            vector,
            whole,
            whole,
            whole,
            whole,
            whole,
            whole,
        ),
        check_vma=False,
    )
```

```python
from functools import partial
import math

import jax
import jax.numpy as jnp
from jax import lax
from jax.experimental import pallas as pl
from jax.experimental.pallas import tpu as pltpu
from jax.sharding import PartitionSpec as P

HS = 128
CROP = 512


EPSILON = 1e-05


def dot(left, right, left_dim, right_dim):
    return lax.dot_general(
        left,
        right,
        (((left_dim,), (right_dim,)), ((), ())),
        preferred_element_type=jnp.float32,
    )


def unit_rows(rows):
    center = rows - jnp.mean(rows, axis=-1, keepdims=True)
    inverse = lax.rsqrt(jnp.mean(center * center, axis=-1, keepdims=True) + EPSILON)
    return center * inverse, inverse


def unit_rows_back(scaled, unit, inverse):
    inner = scaled - jnp.mean(scaled, axis=-1, keepdims=True)
    return (inner - unit * jnp.mean(scaled * unit, axis=-1, keepdims=True)) * inverse


def low(array):
    return array.astype(jnp.bfloat16)


def attend_kernel(first, live_ref, source_ref, *refs):
    if first:
        gain_ref, shift_ref, *refs = refs
    query_weight, key_weight, value_weight, query_bias, value_bias, *refs = refs
    if first:
        normed_ref, *refs = refs
    query_ref, keys_ref, values_ref, weights_ref, attended_ref, inverse_ref = refs

    @pl.when(pl.program_id(0) < live_ref[0])
    def _():
        if first:
            unit, _ = unit_rows(source_ref[...].astype(jnp.float32))
            normed_ref[...] = low(unit * gain_ref[...] + shift_ref[...])
            normed = normed_ref[...]
        else:
            normed = source_ref[...]
        query_ref[...] = low(dot(normed, query_weight[...], 1, 0) + query_bias[...])
        keys_ref[...] = low(dot(normed, key_weight[...], 1, 0))
        values_ref[...] = low(dot(normed, value_weight[...], 1, 0) + value_bias[...])
        ones = jnp.ones((CROP, HS), jnp.bfloat16)
        for head in range(query_ref.shape[1] // HS):
            columns = pl.ds(head * HS, HS)
            scores = dot(query_ref[:, columns], keys_ref[:, columns], 1, 1)
            highest = jnp.max(scores, axis=-1, keepdims=True)
            weights = low(jnp.exp2((scores - highest) * (math.log2(math.e) / math.sqrt(HS))))
            weights_ref[head] = weights
            extended = jnp.concatenate([values_ref[:, columns], ones], axis=1)
            mixed = dot(weights, extended, 1, 0)
            inverse = 1.0 / mixed[:, HS:]
            inverse_ref[:, columns] = inverse
            attended_ref[:, columns] = low(mixed[:, :HS] * inverse)


def gelu_pair(before):
    lower = 0.5 + 0.5 * lax.erf(before * math.sqrt(0.5))
    density = jnp.exp2(before * before * (-0.5 * math.log2(math.e)))
    slope = lower + before * density * (1.0 / math.sqrt(2.0 * math.pi))
    return before * lower, slope


def feed_kernel(
    crops,
    live_ref,
    latents_ref,
    cotangent_ref,
    attended_refs,
    out_weights,
    up_weights,
    down_weights,
    up_biases,
    out_bias,
    down_bias,
    gain,
    shift,
    output_ref,
    hidden_grad_ref,
    attended_grads,
    out_grads,
    up_grads,
    down_grads,
    up_bias_grads,
    vectors_ref,
    out_sums,
    up_sums,
    down_sums,
):
    step = pl.program_id(0)

    @pl.when(step == 0)
    def _():
        for sums in (*out_sums, *up_sums, *down_sums, *up_bias_grads, vectors_ref):
            sums[...] = jnp.zeros_like(sums)

    @pl.when(step >= live_ref[0])
    def _():
        output_ref[...] = jnp.zeros_like(output_ref)
        hidden_grad_ref[...] = jnp.zeros_like(hidden_grad_ref)

    @pl.when(step < live_ref[0])
    def _():
        hidden = latents_ref[...].astype(jnp.float32) + out_bias[...]
        for part in range(2):
            hidden = hidden + dot(attended_refs[part][...], out_weights[part][...], 1, 0)
        unit, inverse = unit_rows(hidden)
        normed = low(unit * gain[...] + shift[...])
        top = cotangent_ref[...]
        result = hidden + down_bias[...]
        second_grad = jnp.zeros(hidden.shape, jnp.float32)
        for part in range(2):
            before = dot(normed, up_weights[part][...], 1, 0) + up_biases[part][...]
            value, slope = gelu_pair(before)
            activated = low(value)
            result = result + dot(activated, down_weights[part][...], 1, 0)
            down_sums[part][...] += dot(activated, top, 0, 0)
            activated_grad = dot(top, down_weights[part][...], 1, 1)
            before_grad = low(activated_grad * slope)
            up_bias_grads[part][...] += jnp.sum(
                before_grad.astype(jnp.float32), axis=0, keepdims=True
            )
            up_sums[part][...] += dot(normed, before_grad, 0, 0)
            second_grad = second_grad + dot(before_grad, up_weights[part][...], 1, 1)
        output_ref[...] = low(result)
        top_grad = top.astype(jnp.float32)
        hidden_grad = top_grad + unit_rows_back(second_grad * gain[...], unit, inverse)
        hidden_grad_ref[...] = hidden_grad
        hidden_low = low(hidden_grad)
        for part in range(2):
            out_sums[part][...] += dot(attended_refs[part][...], hidden_low, 0, 0)
            attended_grads[part][...] = low(dot(hidden_low, out_weights[part][...], 1, 1))
        for row, term in enumerate((second_grad * unit, second_grad, hidden_grad, top_grad)):
            vectors_ref[row : row + 1] += jnp.sum(term, axis=0, keepdims=True)

    @pl.when(step == crops - 1)
    def _():
        for part in range(2):
            out_grads[part][...] = low(out_sums[part][...])
            up_grads[part][...] = low(up_sums[part][...])
            down_grads[part][...] = low(down_sums[part][...])


def attend_back_kernel(
    crops,
    live_ref,
    normed_ref,
    queries,
    keys,
    values,
    weights,
    inverses,
    attended,
    attended_grads,
    matrices,
    query_grads,
    keys_grads,
    values_grads,
    matrix_grads,
    bias_grads,
    gain_terms,
    shift_terms,
    matrix_sums,
):
    step = pl.program_id(0)
    scale = 1.0 / math.sqrt(HS)

    @pl.when(step == 0)
    def _():
        for part in range(2):
            bias_grads[part][...] = jnp.zeros_like(bias_grads[part])
            for kind in range(3):
                matrix_sums[kind][part][...] = jnp.zeros_like(matrix_sums[kind][part])

    @pl.when(step < live_ref[0])
    def _():
        normed = normed_ref[...]
        for part in range(2):
            for head in range(queries[part].shape[1] // HS):
                columns = pl.ds(head * HS, HS)
                inner = attended_grads[part][:, columns].astype(jnp.float32)
                inner = inner * inverses[part][:, columns]
                upstream = low(inner)
                total = jnp.sum(
                    inner * attended[part][:, columns].astype(jnp.float32), axis=1, keepdims=True
                )
                head_weights = weights[part][head]
                values_grads[part][:, columns] = low(dot(head_weights, upstream, 0, 0))
                probs_grad = dot(upstream, values[part][:, columns], 1, 1)
                scores_grad = low(head_weights.astype(jnp.float32) * (probs_grad - total))
                query_grads[part][:, columns] = low(
                    dot(scores_grad, keys[part][:, columns], 1, 0) * scale
                )
                keys_grads[part][:, columns] = low(
                    dot(scores_grad, queries[part][:, columns], 0, 0) * scale
                )
            for kind, grads in enumerate((query_grads, keys_grads, values_grads)):
                grad = grads[part][...]
                matrix_sums[kind][part][...] += dot(normed, grad, 0, 0)
                bias_grads[part][kind : kind + 1] += jnp.sum(
                    grad.astype(jnp.float32), axis=0, keepdims=True
                )

    @pl.when(step == crops - 1)
    def _():
        gain_terms[...] = jnp.zeros_like(gain_terms)
        shift_terms[...] = jnp.zeros_like(shift_terms)
        for part in range(2):
            for kind in range(3):
                matrix = matrices[kind][part]
                sums = matrix_sums[kind][part]
                matrix_grads[kind][part][...] = low(sums[...])
                for start in range(0, matrix.shape[1], HS):
                    columns = pl.ds(start, HS)
                    gain_terms[...] += sums[:, columns] * matrix[:, columns].astype(jnp.float32)
                bias = bias_grads[part][kind : kind + 1]
                rough = low(bias)
                fine = low(bias - rough.astype(jnp.float32))
                shift_terms[...] += dot(
                    jnp.concatenate([rough, fine] + [jnp.zeros_like(rough)] * 6, axis=0),
                    matrix[...],
                    1,
                    1,
                )


def latents_kernel(
    live_ref, latents_ref, hidden_grad_ref, grads, matrices, gain_ref, output_ref
):
    @pl.when(pl.program_id(0) >= live_ref[0])
    def _():
        output_ref[...] = jnp.zeros_like(output_ref)

    @pl.when(pl.program_id(0) < live_ref[0])
    def _():
        unit, inverse = unit_rows(latents_ref[...].astype(jnp.float32))
        upstream = jnp.zeros(output_ref.shape, jnp.float32)
        for kind in range(3):
            for grad, matrix in zip(grads[kind], matrices[kind]):
                upstream = upstream + dot(grad[...], matrix[...], 1, 1)
        output_ref[...] = hidden_grad_ref[...] + unit_rows_back(
            upstream * gain_ref[...], unit, inverse
        )


VMEM_LIMIT = 66_000_000


def row_block(width, column=0):
    return pl.BlockSpec((CROP, width), lambda i, live: (i, column))


def fixed(rows, width, column=0):
    return pl.BlockSpec((rows, width), lambda i, live: (0, column), pipeline_mode=pl.Buffered(1))


def shaped(shape, dtype=jnp.bfloat16):
    return jax.ShapeDtypeStruct(shape, dtype)


def run(kernel, name, crops, in_specs, out_specs, out_shape, flops, moved, scratch=()):
    return pl.pallas_call(
        kernel,
        name=name,
        out_shape=out_shape,
        grid_spec=pltpu.PrefetchScalarGridSpec(
            num_scalar_prefetch=1,
            grid=(crops,),
            in_specs=in_specs,
            out_specs=out_specs,
            scratch_shapes=scratch,
        ),
        compiler_params=pltpu.CompilerParams(
            dimension_semantics=("arbitrary",), vmem_limit_bytes=VMEM_LIMIT
        ),
        cost_estimate=pl.CostEstimate(flops=flops, bytes_accessed=moved, transcendentals=0),
    )


def attend(live, source, norm, matrices, biases):
    count, width = source.shape
    crops = count // CROP
    units = matrices[0].shape[1]
    heads = units // HS
    first = norm is not None
    vector = fixed(1, units)
    outs = (row_block(width),) * first + (
        row_block(units),
        row_block(units),
        row_block(units),
        pl.BlockSpec((None, heads, CROP, CROP), lambda i, live: (i, 0, 0, 0)),
        row_block(units),
        row_block(units),
    )
    rows = shaped((count, units))
    shapes = (shaped((count, width)),) * first + (
        rows,
        rows,
        rows,
        shaped((crops, heads, CROP, CROP)),
        rows,
        shaped((count, units), jnp.float32),
    )
    return run(
        partial(attend_kernel, first),
        "attend_first" if first else "attend_rest",
        crops,
        (row_block(width),)
        + (fixed(1, width),) * (2 * first)
        + (fixed(width, units),) * 3
        + (vector,) * 2,
        outs,
        shapes,
        2 * count * units * (3 * width + 2 * CROP),
        count * (units * (12 + 2 * CROP // HS) + 4 * width),
    )(live, source, *(norm or ()), *matrices, *biases)


def feed(live, latents, cotangent, attended, outs, ups, downs, up_biases, vectors):
    count, width = latents.shape
    crops = count // CROP
    units = [array.shape[1] for array in attended]
    both = lambda make: tuple(make(size) for size in units)
    row_in = both(row_block)
    tall = both(lambda size: fixed(size, width))
    flat = both(lambda size: fixed(width, size))
    thin = both(lambda size: fixed(1, size))
    vector = fixed(1, width)
    sums = lambda dtype: (
        both(lambda size: dtype((size, width))),
        both(lambda size: dtype((width, size))),
        both(lambda size: dtype((size, width))),
    )
    return run(
        partial(feed_kernel, crops),
        "feed",
        crops,
        (row_block(width), row_block(width), row_in, tall, flat, tall, thin)
        + (vector,) * 4,
        (row_block(width), row_block(width), row_in, tall, flat, tall, thin, fixed(8, width)),
        (
            shaped((count, width)),
            shaped((count, width), jnp.float32),
            both(lambda size: shaped((count, size))),
            *sums(shaped),
            both(lambda size: shaped((1, size), jnp.float32)),
            shaped((8, width), jnp.float32),
        ),
        2 * count * width * width * 9,
        count * width * 14,
        sums(lambda shape: pltpu.VMEM(shape, jnp.float32)),
    )(live, latents, cotangent, attended, outs, ups, downs, up_biases, *vectors)


def attend_back(live, normed, saved, attended_grads, matrices, widths, phase):
    count, width = normed.shape
    crops = count // CROP
    both = lambda make: tuple(make(size) for size in widths)
    rows = both(lambda size: row_block(size, phase))
    heads = both(
        lambda size: pl.BlockSpec(
            (None, size // HS, CROP, CROP), lambda i, live: (i, phase, 0, 0)
        )
    )
    flat = both(lambda size: fixed(width, size, phase))
    plain = both(lambda size: fixed(width, size))
    queries, keys, values, weights, attended, inverses = saved
    return run(
        partial(attend_back_kernel, crops),
        "attend_back",
        crops,
        (row_block(width), rows, rows, rows, heads, rows, rows, rows, (flat,) * 3),
        (
            both(row_block),
            both(row_block),
            both(row_block),
            (plain,) * 3,
            both(lambda size: fixed(8, size)),
            fixed(width, HS),
            fixed(8, width),
        ),
        (
            both(lambda size: shaped((count, size))),
            both(lambda size: shaped((count, size))),
            both(lambda size: shaped((count, size))),
            (both(lambda size: shaped((width, size))),) * 3,
            both(lambda size: shaped((8, size), jnp.float32)),
            shaped((width, HS), jnp.float32),
            shaped((8, width), jnp.float32),
        ),
        2 * count * sum(widths) * (3 * width + 4 * CROP),
        count * (sum(widths) * (18 + 2 * CROP // HS) + 2 * width),
        ((both(lambda size: pltpu.VMEM((width, size), jnp.float32)),) * 3,),
    )(
        live,
        normed,
        queries,
        keys,
        values,
        weights,
        inverses,
        attended,
        attended_grads,
        matrices,
    )


def latents_back(live, latents, hidden_grad, grads, matrices, gain):
    count, width = latents.shape
    rows = tuple(tuple(row_block(array.shape[1]) for array in kind) for kind in grads)
    flat = tuple(
        tuple(fixed(width, grad.shape[1], column) for grad, (_, column) in zip(*kinds))
        for kinds in zip(grads, matrices)
    )
    return run(
        latents_kernel,
        "latents_back",
        count // CROP,
        (row_block(width), row_block(width), rows, flat, fixed(1, width)),
        row_block(width),
        shaped((count, width), jnp.float32),
        2 * count * width * width * 3,
        count * width * 16,
    )(
        live,
        latents,
        hidden_grad,
        grads,
        tuple(tuple(array for array, _ in kind) for kind in matrices),
        gain,
    )


def pair_perm(size, bit):
    return [(i, i ^ bit) for i in range(size)]


class Links:
    def __init__(self):
        self.wide = lax.axis_size("wide")
        self.narrow = lax.axis_size("narrow")
        self.paired = self.narrow == 2 and self.wide == 16
        self.index = lax.axis_index("wide")
        self.core = self.index % 2

    def swap(self, array, bit):
        return lax.ppermute(array, "wide", pair_perm(self.wide, bit))

    def swap_narrow(self, array):
        return lax.ppermute(array, "narrow", [(0, 1), (1, 0)])

    def others(self, weight, axis):
        if not self.paired:
            whole = lax.all_gather(weight, "narrow", axis=0, tiled=False)
            whole = jnp.roll(whole, -lax.axis_index("narrow"), axis=0)[1:]
            return jnp.concatenate([whole[i] for i in range(self.narrow - 1)], axis=axis)
        half = weight.shape[0] // 2
        mine = lax.dynamic_slice_in_dim(weight, self.core * half, half, 0)
        near = self.swap_narrow(mine)
        far = self.swap(near, 1)
        first = jnp.where(self.core == 0, near, far)
        second = jnp.where(self.core == 0, far, near)
        return jnp.concatenate([first, second], axis=0)

    def halves(self, array, bit):
        half = array.shape[0] // 2
        position = (self.index // bit) % 2
        keep = lax.dynamic_slice_in_dim(array, position * half, half, 0)
        give = lax.dynamic_slice_in_dim(array, (1 - position) * half, half, 0)
        return keep, give

    def add(self, left, right):
        return (left.astype(jnp.float32) + right.astype(jnp.float32)).astype(jnp.bfloat16)

    def join(self, mine, other, bit):
        position = (self.index // bit) % 2
        first = jnp.where(position == 0, mine, other)
        second = jnp.where(position == 0, other, mine)
        return jnp.concatenate([first, second], axis=0)

    def reduce_matrix(self, own, other, axis):
        own = own.astype(jnp.bfloat16)
        other = other.astype(jnp.bfloat16)
        if not self.paired:
            width = own.shape[axis]
            parts = jnp.stack(
                [own]
                + [
                    lax.slice_in_dim(other, i * width, (i + 1) * width, axis=axis)
                    for i in range(self.narrow - 1)
                ]
            )
            parts = jnp.roll(parts, lax.axis_index("narrow"), axis=0)
            mine = lax.psum_scatter(parts, "narrow", scatter_dimension=0, tiled=True)[0]
            return lax.psum(mine, "wide").astype(jnp.float32)
        keep_own, give_own = self.halves(own, 1)
        keep_other, give_other = self.halves(other, 1)
        keep_other = self.add(keep_other, self.swap(give_other, 1))
        keep = self.add(keep_own, self.swap(give_own, 1))
        keep = self.add(keep, self.swap_narrow(keep_other))
        for bit in (2, 4, 8):
            keep, give = self.halves(keep, bit)
            keep = self.add(keep, self.swap(give, bit))
        for bit in (8, 4, 2, 1):
            keep = self.join(keep, self.swap(keep, bit), bit)
        return keep.astype(jnp.float32)

    def reduce_all(self, rows):
        if not self.paired:
            return lax.psum(rows, ("wide", "narrow"))
        rows = rows + self.swap(rows, 1)
        rows = rows + self.swap_narrow(rows)
        for bit in (2, 4, 8):
            rows = rows + self.swap(rows, bit)
        return rows


def on_device(
    latents,
    cotangent,
    crop_counts,
    image_device,
    query_weight,
    key_weight,
    value_weight,
    out_weight,
    up_weight,
    down_weight,
    query_bias,
    value_bias,
    up_bias,
    out_bias,
    down_bias,
    first_gain,
    first_shift,
    second_gain,
    second_shift,
):
    links = Links()
    count = latents.shape[0]
    width = latents.shape[1]
    narrow = links.narrow
    place = lax.axis_index("narrow")
    owned = jnp.sum(jnp.where(image_device == lax.axis_index("wide"), crop_counts, 0))
    live = (owned - place * (count // CROP)).astype(jnp.int32).reshape(1)
    units = query_weight.shape[1]
    biases = jnp.stack([query_bias, value_bias, up_bias])
    if links.paired:
        biases = jnp.concatenate([biases, links.swap_narrow(biases)], axis=1)
    else:
        biases = lax.all_gather(biases, "narrow", axis=0)
        biases = jnp.roll(biases, -place, axis=0).transpose(1, 0, 2).reshape(3, -1)
    biases = biases.astype(jnp.float32)
    both = lambda row: (biases[row : row + 1, :units], biases[row : row + 1, units:])
    query_biases, value_biases, up_biases = both(0), both(1), both(2)
    vector = lambda array: array.reshape(1, -1)
    queries = (query_weight, links.others(query_weight, 1))
    keys = (key_weight, links.others(key_weight, 1))
    values = (value_weight, links.others(value_weight, 1))
    outs = (out_weight, links.others(out_weight, 0))
    ups = (up_weight, links.others(up_weight, 1))
    downs = (down_weight, links.others(down_weight, 0))

    norm = (vector(first_gain), vector(first_shift))
    matrices = (queries, keys, values)
    first, *saved_own = attend(
        live,
        latents,
        norm,
        [kind[0] for kind in matrices],
        (query_biases[0], value_biases[0]),
    )
    saved_rest = attend(
        live,
        first,
        None,
        [kind[1] for kind in matrices],
        (query_biases[1], value_biases[1]),
    )
    saved = tuple(zip(saved_own, saved_rest))
    (
        block_output,
        hidden_grad,
        attended_grads,
        out_grads,
        up_grads,
        down_grads,
        up_bias_grads,
        feed_vectors,
    ) = feed(
        live,
        latents,
        cotangent,
        saved[4],
        outs,
        ups,
        downs,
        up_biases,
        [vector(array) for array in (out_bias, down_bias, second_gain, second_shift)],
    )
    phases = 2 if links.paired else 1
    widths = (units // phases, (width - units) // phases)
    steps = [
        attend_back(live, first, saved, attended_grads, matrices, widths, phase)
        for phase in range(phases)
    ]
    grads = tuple(
        tuple(array for step in steps for array in step[kind]) for kind in range(3)
    )
    parts = tuple(
        tuple((kind[part], phase) for phase in range(phases) for part in range(2))
        for kind in matrices
    )
    latents_gradient = latents_back(live, latents, hidden_grad, grads, parts, norm[0])

    gain_terms = sum(step[5] for step in steps).sum(axis=1)
    first_shift_grad = sum(step[6] for step in steps).sum(axis=0)
    first_gain_grad = (gain_terms - first_shift * first_shift_grad) / first_gain

    def shared_units(own, rest):
        if narrow == 2:
            ahead = place == 0
            return jnp.where(
                ahead, jnp.concatenate([own, rest]), jnp.concatenate([rest, own])
            )
        return jnp.roll(
            jnp.concatenate([own, rest]).reshape(narrow, units), place, axis=0
        ).reshape(-1)

    def bias_row(kind):
        return shared_units(
            jnp.concatenate([step[4][0][kind] for step in steps]),
            jnp.concatenate([step[4][1][kind] for step in steps]),
        )

    rows = jnp.stack(
        [
            first_gain_grad,
            first_shift_grad,
            *(feed_vectors[row] for row in range(4)),
            bias_row(0),
            bias_row(2),
            shared_units(up_bias_grads[0][0], up_bias_grads[1][0]),
        ]
    )
    rowwise = links.reduce_all(rows)
    own = lax.dynamic_slice_in_dim(rowwise[6:], place * units, units, 1)
    wide_grad = lambda kind: links.reduce_matrix(
        jnp.concatenate([step[3][kind][0] for step in steps], axis=1),
        jnp.concatenate([step[3][kind][1] for step in steps], axis=1),
        1,
    )
    return (
        block_output,
        latents_gradient,
        wide_grad(0),
        wide_grad(1),
        wide_grad(2),
        links.reduce_matrix(*out_grads, 0),
        links.reduce_matrix(*up_grads, 1),
        links.reduce_matrix(*down_grads, 0),
        own[0],
        own[1],
        own[2],
        rowwise[4],
        rowwise[5],
        rowwise[0],
        rowwise[1],
        rowwise[2],
        rowwise[3],
    )


def solution(mesh):
    rows = P(("wide", "narrow"), None)
    columns = P(None, "narrow")
    units = P("narrow", None)
    vector = P("narrow")
    whole = P()
    return jax.shard_map(
        on_device,
        mesh=mesh,
        in_specs=(
            rows,
            rows,
            whole,
            whole,
            columns,
            columns,
            columns,
            units,
            columns,
            units,
            vector,
            vector,
            vector,
            whole,
            whole,
            whole,
            whole,
            whole,
            whole,
        ),
        out_specs=(
            rows,
            rows,
            columns,
            columns,
            columns,
            units,
            columns,
            units,
            vector,
            vector,
            vector,
            whole,
            whole,
            whole,
            whole,
            whole,
            whole,
        ),
        check_vma=False,
    )
```

```python
from functools import partial
import math

import jax
import jax.numpy as jnp
from jax import lax
from jax.experimental import pallas as pl
from jax.experimental.pallas import tpu as pltpu
from jax.sharding import PartitionSpec as P

HS = 128
CROP = 512


EPSILON = 1e-05


def dot(left, right, left_dim, right_dim):
    return lax.dot_general(
        left,
        right,
        (((left_dim,), (right_dim,)), ((), ())),
        preferred_element_type=jnp.float32,
    )


def unit_rows(rows):
    center = rows - jnp.mean(rows, axis=-1, keepdims=True)
    inverse = lax.rsqrt(jnp.mean(center * center, axis=-1, keepdims=True) + EPSILON)
    return center * inverse, inverse


def unit_rows_back(scaled, unit, inverse):
    inner = scaled - jnp.mean(scaled, axis=-1, keepdims=True)
    return (inner - unit * jnp.mean(scaled * unit, axis=-1, keepdims=True)) * inverse


def low(array):
    return array.astype(jnp.bfloat16)


def attend_kernel(first, live_ref, source_ref, *refs):
    if first:
        gain_ref, shift_ref, *refs = refs
    query_weight, key_weight, value_weight, query_bias, value_bias, *refs = refs
    if first:
        normed_ref, *refs = refs
    query_ref, keys_ref, values_ref, weights_ref, attended_ref, inverse_ref = refs

    @pl.when(pl.program_id(0) < live_ref[0])
    def _():
        if first:
            unit, _ = unit_rows(source_ref[...].astype(jnp.float32))
            normed_ref[...] = low(unit * gain_ref[...] + shift_ref[...])
            normed = normed_ref[...]
        else:
            normed = source_ref[...]
        query_ref[...] = low(dot(normed, query_weight[...], 1, 0) + query_bias[...])
        keys_ref[...] = low(dot(normed, key_weight[...], 1, 0))
        values_ref[...] = low(dot(normed, value_weight[...], 1, 0) + value_bias[...])
        ones = jnp.ones((CROP, HS), jnp.bfloat16)
        for head in range(query_ref.shape[1] // HS):
            columns = pl.ds(head * HS, HS)
            scores = dot(query_ref[:, columns], keys_ref[:, columns], 1, 1)
            highest = jnp.max(scores, axis=-1, keepdims=True)
            weights = low(jnp.exp2((scores - highest) * (math.log2(math.e) / math.sqrt(HS))))
            weights_ref[head] = weights
            extended = jnp.concatenate([values_ref[:, columns], ones], axis=1)
            mixed = dot(weights, extended, 1, 0)
            inverse = 1.0 / mixed[:, HS:]
            inverse_ref[:, columns] = inverse
            attended_ref[:, columns] = low(mixed[:, :HS] * inverse)


def gelu_pair(before):
    lower = 0.5 + 0.5 * lax.erf(before * math.sqrt(0.5))
    density = jnp.exp2(before * before * (-0.5 * math.log2(math.e)))
    slope = lower + before * density * (1.0 / math.sqrt(2.0 * math.pi))
    return before * lower, slope


def feed_kernel(
    crops,
    split,
    live_ref,
    latents_ref,
    cotangent_ref,
    attended_refs,
    out_weights,
    up_weights,
    down_weights,
    up_biases,
    out_bias,
    down_bias,
    gain,
    shift,
    output_ref,
    hidden_grad_ref,
    attended_grads,
    packed,
    up_bias_grads,
    vectors_ref,
    out_sums,
    up_sums,
    down_sums,
):
    step = pl.program_id(0)

    @pl.when(step == 0)
    def _():
        for sums in (*out_sums, *up_sums, *down_sums, *up_bias_grads, vectors_ref):
            sums[...] = jnp.zeros_like(sums)

    @pl.when(step >= live_ref[0])
    def _():
        output_ref[...] = jnp.zeros_like(output_ref)
        hidden_grad_ref[...] = jnp.zeros_like(hidden_grad_ref)

    @pl.when(step < live_ref[0])
    def _():
        hidden = latents_ref[...].astype(jnp.float32) + out_bias[...]
        for part in range(2):
            hidden = hidden + dot(attended_refs[part][...], out_weights[part][...], 1, 0)
        unit, inverse = unit_rows(hidden)
        normed = low(unit * gain[...] + shift[...])
        top = cotangent_ref[...]
        result = hidden + down_bias[...]
        second_grad = jnp.zeros(hidden.shape, jnp.float32)
        for part in range(2):
            before = dot(normed, up_weights[part][...], 1, 0) + up_biases[part][...]
            value, slope = gelu_pair(before)
            activated = low(value)
            result = result + dot(activated, down_weights[part][...], 1, 0)
            down_sums[part][...] += dot(activated, top, 0, 0)
            activated_grad = dot(top, down_weights[part][...], 1, 1)
            before_grad = low(activated_grad * slope)
            up_bias_grads[part][...] += jnp.sum(
                before_grad.astype(jnp.float32), axis=0, keepdims=True
            )
            up_sums[part][...] += dot(normed, before_grad, 0, 0)
            second_grad = second_grad + dot(before_grad, up_weights[part][...], 1, 1)
        output_ref[...] = low(result)
        top_grad = top.astype(jnp.float32)
        hidden_grad = top_grad + unit_rows_back(second_grad * gain[...], unit, inverse)
        hidden_grad_ref[...] = hidden_grad
        hidden_low = low(hidden_grad)
        for part in range(2):
            out_sums[part][...] += dot(attended_refs[part][...], hidden_low, 0, 0)
            attended_grads[part][...] = low(dot(hidden_low, out_weights[part][...], 1, 1))
        for row, term in enumerate((second_grad * unit, second_grad, hidden_grad, top_grad)):
            vectors_ref[row : row + 1] += jnp.sum(term, axis=0, keepdims=True)

    @pl.when(step == crops - 1)
    def _():
        if not split:
            for grads, sums in zip(packed, (down_sums, out_sums, up_sums)):
                for part in range(2):
                    grads[part][...] = low(sums[part][...])
            return
        for group, core in zip(packed, (live_ref[1], 1 - live_ref[1])):
            tall_ref, flat_ref = group
            rows = flat_ref.shape[0] // 2
            short = tall_ref.shape[0] // (4 * PIECES)
            half = tall_ref.shape[1] // 2
            for part in range(2):
                flat_ref[part * rows : (part + 1) * rows] = low(
                    up_sums[part][pl.ds(pl.multiple_of(core * rows, rows), rows), :]
                )
                for piece in range(PIECES):
                    start = core * (PIECES * short) + piece * short
                    source = pl.ds(pl.multiple_of(start, short), short)
                    for side in range(2):
                        base = part * rows + (2 * piece + side) * short
                        across = pl.ds(side * half, half)
                        for index, sums in enumerate((down_sums, out_sums)):
                            tall_ref[base : base + short, index * half : (index + 1) * half] = low(
                                sums[part][source, across]
                            )


def attend_back_kernel(
    crops,
    split,
    live_ref,
    normed_ref,
    queries,
    keys,
    values,
    weights,
    inverses,
    attended,
    attended_grads,
    matrices,
    previous,
    packed_before,
    grads,
    packed,
    bias_grads,
    gain_terms,
    shift_terms,
    joined,
    sums,
):
    step = pl.program_id(0)
    scale = 1.0 / math.sqrt(HS)
    widths = [ref.shape[1] for ref in queries]
    bases = (0, 3 * widths[0])

    @pl.when(step == 0)
    def _():
        sums[...] = jnp.zeros_like(sums)
        for part in range(2):
            bias_grads[part][...] = jnp.zeros_like(bias_grads[part])

    @pl.when(step < live_ref[0])
    def _():
        for part in range(2):
            for head in range(widths[part] // HS):
                columns = pl.ds(head * HS, HS)

                def put(kind, value):
                    value = low(value)
                    grads[kind][part][:, columns] = value
                    joined[:, pl.ds(bases[part] + kind * widths[part] + head * HS, HS)] = value

                inner = attended_grads[part][:, columns].astype(jnp.float32)
                inner = inner * inverses[part][:, columns]
                upstream = low(inner)
                total = jnp.sum(
                    inner * attended[part][:, columns].astype(jnp.float32), axis=1, keepdims=True
                )
                head_weights = weights[part][head]
                put(2, dot(head_weights, upstream, 0, 0))
                probs_grad = dot(upstream, values[part][:, columns], 1, 1)
                scores_grad = low(head_weights.astype(jnp.float32) * (probs_grad - total))
                put(0, dot(scores_grad, keys[part][:, columns], 1, 0) * scale)
                put(1, dot(scores_grad, queries[part][:, columns], 0, 0) * scale)
            for kind in range(3):
                bias_grads[part][kind : kind + 1] += jnp.sum(
                    grads[kind][part][...].astype(jnp.float32), axis=0, keepdims=True
                )
        sums[...] += dot(normed_ref[...], joined[...], 0, 0)

    @pl.when(step == crops - 1)
    def _():
        gain_terms[...] = jnp.zeros_like(gain_terms)
        shift_terms[...] = jnp.zeros_like(shift_terms)
        for part in range(2):
            for kind in range(3):
                matrix = matrices[kind][part]
                base = bases[part] + kind * widths[part]
                for start in range(0, widths[part], HS):
                    gain_terms[...] += sums[:, pl.ds(base + start, HS)] * matrix[
                        :, pl.ds(start, HS)
                    ].astype(jnp.float32)
                bias = bias_grads[part][kind : kind + 1]
                rough = low(bias)
                fine = low(bias - rough.astype(jnp.float32))
                shift_terms[...] += dot(
                    jnp.concatenate([rough, fine] + [jnp.zeros_like(rough)] * 6, axis=0),
                    matrix[...],
                    1,
                    1,
                )
        if not split:
            packed[0][...] = low(sums[...])
            return
        half = sums.shape[0] // 2
        for target, core in zip(packed, (live_ref[1], 1 - live_ref[1])):
            rows = pl.ds(pl.multiple_of(core * half, half), half)
            for part in range(2):
                target[part * half : (part + 1) * half] = low(
                    sums[rows, pl.ds(bases[part], 3 * widths[part])]
                )


def latents_kernel(
    first, live_ref, latents_ref, hidden_grad_ref, grads, matrices, gain_ref, previous, output_ref
):
    crop = pl.program_id(0) + first

    @pl.when(crop >= live_ref[0])
    def _():
        output_ref[...] = jnp.zeros_like(output_ref)

    @pl.when(crop < live_ref[0])
    def _():
        unit, inverse = unit_rows(latents_ref[...].astype(jnp.float32))
        upstream = jnp.zeros(output_ref.shape, jnp.float32)
        for kind in range(3):
            for grad, matrix in zip(grads[kind], matrices[kind]):
                upstream = upstream + dot(grad[...], matrix[...], 1, 1)
        output_ref[...] = hidden_grad_ref[...] + unit_rows_back(
            upstream * gain_ref[...], unit, inverse
        )


def finish_kernel(places_ref, groups, *outputs):
    for half, group in enumerate(groups):
        for index, source in enumerate(group):
            pieces = 16 // len(group)
            size = source.shape[0] // pieces
            width = source.shape[1] // 6
            for piece in range(pieces):
                start = pl.multiple_of(places_ref[index * pieces + piece] * size, size)
                for column in range(6):
                    phase, kind = 2 * half + column // 3, column % 3
                    outputs[kind][pl.ds(start, size), pl.ds(phase * width, width)] = source[
                        piece * size : (piece + 1) * size, pl.ds(column * width, width)
                    ].astype(jnp.float32)


def finish_feed_kernel(places_ref, sources, down_ref, out_ref, up_ref):
    half = up_ref.shape[1]
    for index, source in enumerate(sources):
        pieces = 16 // len(sources)
        size = source.shape[0] // pieces
        short = size // 2
        for piece in range(pieces):
            place = places_ref[index * pieces + piece]
            up_ref[pl.ds(pl.multiple_of(place * size, size), size), :] = source[
                piece * size : (piece + 1) * size, pl.ds(2 * half, half)
            ].astype(jnp.float32)
            rows = pl.ds(pl.multiple_of(place * short, short), short)
            for side in range(2):
                start = piece * size + side * short
                for column, target in enumerate((down_ref, out_ref)):
                    target[rows, pl.ds(side * half, half)] = source[
                        start : start + short, pl.ds(column * half, half)
                    ].astype(jnp.float32)


def rows_kernel(
    place_ref, gains, shifts, biases, feed_vectors, up_biases, gain_ref, shift_ref, rows_ref
):
    gain_terms = gains[0][...]
    shift_terms = shifts[0][...]
    for more in gains[1:]:
        gain_terms = gain_terms + more[...]
    for more in shifts[1:]:
        shift_terms = shift_terms + more[...]
    shift_grad = jnp.sum(shift_terms, axis=0, keepdims=True)
    unscaled = jnp.sum(gain_terms.T, axis=0, keepdims=True)
    rows_ref[...] = jnp.zeros_like(rows_ref)
    rows_ref[0:1] = (unscaled - shift_ref[...] * shift_grad) / gain_ref[...]
    rows_ref[1:2] = shift_grad
    rows_ref[2:6] = feed_vectors[0:4]

    def put(row, own, rest):
        own = jnp.concatenate(own, axis=1)
        rest = jnp.concatenate(rest, axis=1)
        rows_ref[row : row + 1] = jnp.where(
            place_ref[0] == 0,
            jnp.concatenate([own, rest], axis=1),
            jnp.concatenate([rest, own], axis=1),
        )

    for row, kind in ((6, 0), (7, 2)):
        put(row, *([pair[part][kind : kind + 1] for pair in biases] for part in range(2)))
    put(8, *([array[...]] for array in up_biases))


PIECES = 8
VMEM_LIMIT = 66_000_000
COST_SCALE = 8


def row_block(width, column=0):
    return pl.BlockSpec((CROP, width), lambda i, live: (i, column))


def fixed(rows, width, column=0):
    return pl.BlockSpec((rows, width), lambda i, live: (0, column), pipeline_mode=pl.Buffered(1))


def shaped(shape, dtype=jnp.bfloat16):
    return jax.ShapeDtypeStruct(shape, dtype)


def run(
    kernel, name, crops, in_specs, out_specs, out_shape, flops, moved, scratch=(), aliases=None
):
    return pl.pallas_call(
        kernel,
        input_output_aliases=aliases or {},
        name=name,
        out_shape=out_shape,
        grid_spec=pltpu.PrefetchScalarGridSpec(
            num_scalar_prefetch=1,
            grid=(crops,),
            in_specs=in_specs,
            out_specs=out_specs,
            scratch_shapes=scratch,
        ),
        compiler_params=pltpu.CompilerParams(
            dimension_semantics=("arbitrary",), vmem_limit_bytes=VMEM_LIMIT
        ),
        cost_estimate=pl.CostEstimate(
            flops=COST_SCALE * flops, bytes_accessed=COST_SCALE * moved, transcendentals=0
        ),
    )


def attend(live, source, norm, matrices, biases):
    count, width = source.shape
    crops = count // CROP
    units = matrices[0].shape[1]
    heads = units // HS
    first = norm is not None
    vector = fixed(1, units)
    outs = (row_block(width),) * first + (
        row_block(units),
        row_block(units),
        row_block(units),
        pl.BlockSpec((None, heads, CROP, CROP), lambda i, live: (i, 0, 0, 0)),
        row_block(units),
        row_block(units),
    )
    rows = shaped((count, units))
    shapes = (shaped((count, width)),) * first + (
        rows,
        rows,
        rows,
        shaped((crops, heads, CROP, CROP)),
        rows,
        shaped((count, units), jnp.float32),
    )
    return run(
        partial(attend_kernel, first),
        "attend_first" if first else "attend_rest",
        crops,
        (row_block(width),)
        + (fixed(1, width),) * (2 * first)
        + (fixed(width, units),) * 3
        + (vector,) * 2,
        outs,
        shapes,
        2 * count * units * (3 * width + 2 * CROP),
        count * (units * (12 + 2 * CROP // HS) + 4 * width),
    )(live, source, *(norm or ()), *matrices, *biases)


def feed(live, latents, cotangent, attended, outs, ups, downs, up_biases, vectors, split):
    count, width = latents.shape
    crops = count // CROP
    units = [array.shape[1] for array in attended]
    both = lambda make: tuple(make(size) for size in units)
    row_in = both(row_block)
    tall = both(lambda size: fixed(size, width))
    flat = both(lambda size: fixed(width, size))
    thin = both(lambda size: fixed(1, size))
    vector = fixed(1, width)
    sums = lambda dtype: (
        both(lambda size: dtype((size, width))),
        both(lambda size: dtype((width, size))),
        both(lambda size: dtype((size, width))),
    )
    if split:
        packed_specs = ((fixed(width, width), fixed(width, width // 2)),) * 2
        packed_shapes = ((shaped((width, width)), shaped((width, width // 2))),) * 2
    else:
        packed_specs = (tall, tall, flat)
        out_shapes, up_shapes, down_shapes = sums(shaped)
        packed_shapes = (down_shapes, out_shapes, up_shapes)
    return run(
        partial(feed_kernel, crops, split),
        "feed",
        crops,
        (row_block(width), row_block(width), row_in, tall, flat, tall, thin)
        + (vector,) * 4,
        (row_block(width), row_block(width), row_in, packed_specs, thin, fixed(8, width)),
        (
            shaped((count, width)),
            shaped((count, width), jnp.float32),
            both(lambda size: shaped((count, size))),
            packed_shapes,
            both(lambda size: shaped((1, size), jnp.float32)),
            shaped((8, width), jnp.float32),
        ),
        2 * count * width * width * 9,
        count * width * 14,
        sums(lambda shape: pltpu.VMEM(shape, jnp.float32)),
    )(live, latents, cotangent, attended, outs, ups, downs, up_biases, *vectors)


def attend_back(
    live, normed, saved, attended_grads, matrices, widths, phase, previous, packed_before, split
):
    count, width = normed.shape
    crops = count // CROP
    both = lambda make: tuple(make(size) for size in widths)
    units = [array.shape[1] for array in saved[0]]
    rows = both(lambda size: row_block(size, phase))
    heads = both(
        lambda size: pl.BlockSpec(
            (None, size // HS, CROP, CROP), lambda i, live: (i, phase, 0, 0)
        )
    )
    flat = both(lambda size: fixed(width, size, phase))
    queries, keys, values, weights, attended, inverses = saved
    joined = 3 * sum(widths)
    if split:
        packed_specs = (fixed(width, joined // 2, phase % 2),) * 2
        packed_shapes = (shaped((width, joined)),) * 2
    else:
        packed_specs = (fixed(width, joined),)
        packed_shapes = (shaped((width, joined)),)
    operands = (
        live,
        normed,
        queries,
        keys,
        values,
        weights,
        inverses,
        attended,
        attended_grads,
        matrices,
    )
    before = len(jax.tree.leaves(operands))
    carried = len(jax.tree.leaves(previous))
    aliases = {before + i: i for i in range(carried)}
    for i in range(len(packed_before)):
        aliases[before + carried + i] = 6 + i
    untouched = lambda arrays: jax.tree.map(lambda _: pl.BlockSpec(memory_space=pl.ANY), arrays)
    return run(
        partial(attend_back_kernel, crops, split),
        "attend_back",
        crops,
        (row_block(width), rows, rows, rows, heads, rows, rows, rows, (flat,) * 3)
        + (untouched(previous), untouched(packed_before)),
        (
            (rows,) * 3,
            packed_specs,
            both(lambda size: fixed(8, size)),
            fixed(width, HS),
            fixed(8, width),
        ),
        (
            (tuple(shaped((count, size)) for size in units),) * 3,
            packed_shapes,
            both(lambda size: shaped((8, size), jnp.float32)),
            shaped((width, HS), jnp.float32),
            shaped((8, width), jnp.float32),
        ),
        2 * count * sum(widths) * (3 * width + 4 * CROP),
        count * (sum(widths) * (18 + 2 * CROP // HS) + 2 * width),
        (
            pltpu.VMEM((CROP, joined), jnp.bfloat16),
            pltpu.VMEM((width, joined), jnp.float32),
        ),
        aliases,
    )(*operands, previous, packed_before)


def latents_back(live, latents, hidden_grad, grads, matrices, gain, first, crops, previous):
    count, width = latents.shape
    block = lambda size: pl.BlockSpec((CROP, size), lambda i, live: (i + first, 0))
    rows = tuple(tuple(block(array.shape[1]) for array in kind) for kind in grads)
    flat = tuple(tuple(fixed(*array.shape) for array in kind) for kind in matrices)
    operands = (live, latents, hidden_grad, grads, matrices, gain)
    before = len(jax.tree.leaves(operands))
    return run(
        partial(latents_kernel, first),
        "latents_back",
        crops,
        (block(width), block(width), rows, flat, fixed(1, width))
        + (tuple(pl.BlockSpec(memory_space=pl.ANY) for _ in previous),),
        block(width),
        shaped((count, width), jnp.float32),
        2 * crops * CROP * width * width * 3,
        crops * CROP * width * 16,
        (),
        {before + i: i for i in range(len(previous))},
    )(*operands, previous)


def place_pieces(kernel, name, places, operands, out_shape):
    return pl.pallas_call(
        kernel,
        name=name,
        out_shape=out_shape,
        grid_spec=pltpu.PrefetchScalarGridSpec(
            num_scalar_prefetch=1,
            grid=(1,),
            in_specs=jax.tree.map(
                lambda array: pl.BlockSpec(array.shape, lambda i, places: (0, 0)), operands
            ),
            out_specs=jax.tree.map(
                lambda array: pl.BlockSpec(array.shape, lambda i, places: (0, 0)), out_shape
            ),
        ),
        compiler_params=pltpu.CompilerParams(
            dimension_semantics=("arbitrary",), vmem_limit_bytes=VMEM_LIMIT
        ),
    )(places, *operands)


def pair_perm(size, bit):
    return [(i, i ^ bit) for i in range(size)]


def after(value, *needed):
    return lax.optimization_barrier((value, needed))[0]


class Links:
    def __init__(self):
        self.wide = lax.axis_size("wide")
        self.narrow = lax.axis_size("narrow")
        self.paired = self.narrow == 2 and self.wide == 16
        self.index = lax.axis_index("wide")
        self.core = self.index % 2
        self.across = (self.index // 2) % 2
        self.along = self.index // 4
        self.token = ()
        self.sent = ()

    def slot(self, token):
        self.token = token
        self.sent = ()

    def swap(self, array, bit):
        return lax.ppermute(array, "wide", pair_perm(self.wide, bit))

    def swap_narrow(self, array):
        return lax.ppermute(array, "narrow", [(0, 1), (1, 0)])

    def others(self, weight, axis):
        whole = lax.all_gather(weight, "narrow", axis=0, tiled=False)
        whole = jnp.roll(whole, -lax.axis_index("narrow"), axis=0)[1:]
        return jnp.concatenate([whole[i] for i in range(self.narrow - 1)], axis=axis)

    def joined(self, near, far, index, count, side=None):
        rows = near.shape[0] // count
        columns = slice(None)
        if side is not None:
            width = near.shape[1] // 2
            columns = slice(side * width, (side + 1) * width)
        near, far = (array[index * rows : (index + 1) * rows, columns] for array in (near, far))
        return jnp.concatenate(
            [jnp.where(self.core == 0, near, far), jnp.where(self.core == 0, far, near)], axis=0
        )

    def places(self):
        return jnp.stack(
            [
                (self.core ^ core) * 8 + (self.across ^ across) * 4 + (self.along ^ along)
                for core in range(2)
                for across in range(2)
                for along in (0, 2, 1, 3)
            ]
        ).astype(jnp.int32)

    def reduce_plain(self, own, other, axis):
        width = own.shape[axis]
        parts = jnp.stack(
            [own]
            + [
                lax.slice_in_dim(other, i * width, (i + 1) * width, axis=axis)
                for i in range(self.narrow - 1)
            ]
        )
        parts = jnp.roll(parts, lax.axis_index("narrow"), axis=0)
        mine = lax.psum_scatter(parts, "narrow", scatter_dimension=0, tiled=True)[0]
        return lax.psum(mine, "wide").astype(jnp.float32)


def total(terms, size):
    parts = [
        lax.dynamic_slice_in_dim(array, start, size, 0).astype(jnp.float32)
        for array, start in terms
    ]
    return sum(parts[1:], parts[0]).astype(jnp.bfloat16)


def moved(terms, rows):
    return [(array, start + rows) for array, start in terms]


class Exchange:
    def __init__(self, links):
        self.links = links

    def waiting(self, terms):
        return [(after(array, self.links.token), start) for array, start in terms]

    def exchange(self, arrays, *sends):
        arrays = tuple(after(array, self.links.token) for array in arrays)
        self.links.sent += arrays
        return tuple(send(array) for send, array in zip(sends, arrays))


class Reduction(Exchange):
    def __init__(self, links, keep, give):
        super().__init__(links)
        self.rows = keep.shape[0] // 2
        self.own = [(keep, 0)]
        self.other = [(keep, self.rows)]
        self.give = give

    def cores(self):
        (got,) = self.exchange([self.give], lambda array: self.links.swap(array, 1))
        self.own += [(got, 0)]
        self.other += [(got, self.rows)]

    def narrows(self):
        give = total(self.waiting(self.other), self.rows)
        (got,) = self.exchange([give], self.links.swap_narrow)
        self.own += [(got, 0)]
        self.other = []
        self.got = got

    def acrosses(self):
        size = self.rows // 2
        across = self.links.across
        parts = [self.waiting(terms) for terms in (self.own, self.other) if terms]
        gives = [total(moved(terms, (1 - across) * size), size) for terms in parts]
        give = jnp.concatenate(gives, axis=0) if len(gives) > 1 else gives[0]
        (got,) = self.exchange([give], lambda array: self.links.swap(array, 2))
        self.own = moved(self.own, across * size) + [(got, 0)]
        if self.other:
            self.other = moved(self.other, across * size) + [(got, size)]
        self.rows = size
        self.got = got


class Ending(Exchange):
    def __init__(self, links, groups):
        super().__init__(links)
        self.groups = groups
        self.swaps = [
            lambda array: links.swap(array, 4),
            lambda array: links.swap(array, 8),
            lambda array: links.swap(array, 12),
        ]

    def alongs(self):
        size = self.groups[0].rows // 4
        for group in self.groups:
            group.own = self.waiting(group.own)
        terms = lambda group, bit: moved(group.own, (self.links.along ^ bit) * size)
        gives = [
            jnp.concatenate([total(terms(group, bit), size) for group in self.groups], axis=1)
            for bit in range(1, 4)
        ]
        got = self.exchange(gives, *self.swaps)
        self.parts = [terms(group, 0) for group in self.groups]
        self.size = size
        self.got = got

    def piece(self):
        got = [after(array, self.links.token) for array in self.got]
        pieces = []
        column = 0
        for terms in self.parts:
            width = terms[0][0].shape[1]
            mine = [
                (lax.slice_in_dim(array, column, column + width, axis=1), 0) for array in got
            ]
            pieces.append(total(self.waiting(terms) + mine, self.size))
            column += width
        return jnp.concatenate(pieces, axis=1)

    def along_back(self):
        piece = self.piece()
        self.got = self.exchange([piece] * 3, *self.swaps)
        near, far, opposite = self.got
        self.column = (piece, far, near, opposite)

    def far_back(self):
        piece = self.piece()
        self.got = self.exchange([piece], self.swaps[1])
        self.column = (piece, *self.got)

    def near_back(self):
        column = self.whole_column()
        self.got = self.exchange([column], self.swaps[0])
        self.columns = (column, *self.got)

    def whole_column(self):
        return jnp.concatenate([after(array, self.links.token) for array in self.column], axis=0)

    def across_back(self, columns=None):
        columns = columns or (self.whole_column(),)
        self.got = self.exchange(columns, *(len(columns) * (lambda array: self.links.swap(array, 2),)))
        return (*columns, *self.got)

    def core_back(self, columns):
        swap = lambda array: self.links.swap(array, 1)
        got = self.exchange(columns, *(len(columns) * (swap,)))
        self.result = (*columns, *got)


class SmallSum(Exchange):
    def __init__(self, links, rows):
        super().__init__(links)
        self.rows = rows
        self.left = [
            lambda rows: links.swap(rows, 2),
            lambda rows: links.swap(rows, 1),
            links.swap_narrow,
            lambda rows: links.swap(rows, 4),
            lambda rows: links.swap(rows, 8),
        ]

    def step(self):
        (got,) = self.exchange([self.rows], self.left.pop(0))
        self.rows = self.rows + got


def on_device(
    latents,
    cotangent,
    crop_counts,
    image_device,
    query_weight,
    key_weight,
    value_weight,
    out_weight,
    up_weight,
    down_weight,
    query_bias,
    value_bias,
    up_bias,
    out_bias,
    down_bias,
    first_gain,
    first_shift,
    second_gain,
    second_shift,
):
    links = Links()
    paired = links.paired
    count = latents.shape[0]
    crops = count // CROP
    width = latents.shape[1]
    narrow = links.narrow
    place = lax.axis_index("narrow")
    owned = jnp.sum(jnp.where(image_device == lax.axis_index("wide"), crop_counts, 0))
    live = jnp.stack([owned - place * crops, links.core]).astype(jnp.int32)
    units = query_weight.shape[1]
    biases = jnp.stack([query_bias, value_bias, up_bias])
    if paired:
        rest_biases = links.swap_narrow(biases)
    else:
        rest_biases = lax.all_gather(biases, "narrow", axis=0)
        rest_biases = jnp.roll(rest_biases, -place, axis=0).transpose(1, 0, 2).reshape(3, -1)
        rest_biases = rest_biases[:, units:]
    vector = lambda array: array.reshape(1, -1)
    bias_pair = lambda own, row: (
        vector(own).astype(jnp.float32),
        rest_biases[row : row + 1].astype(jnp.float32),
    )
    query_biases = bias_pair(query_bias, 0)
    value_biases = bias_pair(value_bias, 1)
    up_biases = bias_pair(up_bias, 2)
    norm = (vector(first_gain), vector(first_shift))
    own_weights = (query_weight, key_weight, value_weight)
    if paired:
        half = lambda weight: lax.dynamic_slice_in_dim(
            weight, links.core * (weight.shape[0] // 2), weight.shape[0] // 2, 0
        )
        attend_half = jnp.concatenate([half(weight) for weight in own_weights], axis=0)
        attend_near = links.swap_narrow(attend_half)
    first, *saved_own = attend(
        after(live, attend_half) if paired else live,
        latents,
        norm,
        own_weights,
        (query_biases[0], value_biases[0]),
    )
    if paired:
        up_half = half(after(up_weight, first))
        rows = up_half.shape[0] // 2
        feed_half = jnp.concatenate(
            [
                half(after(out_weight, first)),
                half(after(down_weight, first)),
                jnp.concatenate([up_half[:rows], up_half[rows:]], axis=1),
            ],
            axis=0,
        )
        feed_near = links.swap_narrow(feed_half)
        attend_far = links.swap(after(attend_near, first), 1)
        rest_weights = tuple(links.joined(attend_near, attend_far, i, 3) for i in range(3))
    else:
        rest_weights = tuple(links.others(weight, 1) for weight in own_weights)
    saved_rest = attend(
        after(live, feed_half) if paired else live,
        first,
        None,
        rest_weights,
        (query_biases[1], value_biases[1]),
    )
    if paired:
        feed_near = after(feed_near, saved_rest[0])
        feed_far = links.swap(feed_near, 1)
        rest_out, rest_down = (links.joined(feed_near, feed_far, i, 3) for i in range(2))
        sides = [links.joined(feed_near, feed_far, 2, 3, side) for side in range(2)]
        rest_up = jnp.concatenate(
            [side[start : start + rows] for start in (0, rows) for side in sides], axis=0
        )
    else:
        rest_out = links.others(out_weight, 0)
        rest_up = links.others(up_weight, 1)
        rest_down = links.others(down_weight, 0)
    matrices = tuple(zip(own_weights, rest_weights))
    outs = (out_weight, rest_out)
    ups = (up_weight, rest_up)
    downs = (down_weight, rest_down)
    saved = tuple(zip(saved_own, saved_rest))
    (
        block_output,
        hidden_grad,
        attended_grads,
        feed_packed,
        up_bias_grads,
        feed_vectors,
    ) = feed(
        live,
        latents,
        cotangent,
        saved[4],
        outs,
        ups,
        downs,
        up_biases,
        [vector(array) for array in (out_bias, down_bias, second_gain, second_shift)],
        paired,
    )

    def back(live, phase, widths, previous, packed_before):
        return attend_back(
            live,
            first,
            saved,
            attended_grads,
            matrices,
            widths,
            phase,
            previous,
            packed_before,
            paired,
        )

    def latents_step(live, grads, start, size, previous):
        return latents_back(
            live, latents, hidden_grad, grads, matrices, norm[0], start, size, previous
        )

    if paired:
        phases = units // HS
        widths = (HS, (width - units) // phases)
        ready = lambda: after(live, links.sent)
        tall, flat = (Reduction(links, keep, give) for keep, give in zip(*feed_packed))
        links.slot(feed_vectors)
        tall.cores()
        flat.cores()
        a = back(ready(), 0, widths, (), ())
        links.slot(a[3])
        tall.narrows()
        flat.acrosses()
        b = back(ready(), 1, widths, a[0], a[1])
        early = Reduction(links, *b[1])
        links.slot(b[3])
        flat.narrows()
        early.cores()
        c = back(ready(), 2, widths, b[0], ())
        links.slot(c[3])
        tall.acrosses()
        early.narrows()
        d = back(ready(), 3, widths, c[0], c[1])
        late = Reduction(links, *d[1])
        rows = place_pieces(
            rows_kernel,
            "vector_rows",
            place.astype(jnp.int32).reshape(1),
            (
                tuple(step[3] for step in (a, b, c, d)),
                tuple(step[4] for step in (a, b, c, d)),
                tuple(step[2] for step in (a, b, c, d)),
                feed_vectors,
                up_bias_grads,
                *norm,
            ),
            shaped((16, width), jnp.float32),
        )
        feeds = Ending(links, (tall, flat))
        earlies = Ending(links, (early,))
        lates = Ending(links, (late,))
        small = SmallSum(links, rows)
        top = crops // 2
        links.slot(d[3])
        feeds.alongs()
        early.acrosses()
        late.cores()
        upper = latents_step(ready(), d[0], 0, top, ())
        links.slot(upper)
        feeds.far_back()
        earlies.alongs()
        late.narrows()
        latents_gradient = latents_step(ready(), d[0], top, crops - top, (upper,))
        places = links.places()
        links.slot((latents_gradient, feeds.got, earlies.got))
        late.acrosses()
        feeds.near_back()
        earlies.far_back()
        small.step()
        links.slot((late.got, feeds.got, earlies.got, small.rows, places))
        lates.alongs()
        near_column, far_column = feeds.columns
        near_columns = feeds.across_back((near_column,))
        earlies.near_back()
        links.slot((lates.got, earlies.got, feeds.got))
        lates.along_back()
        far_columns = feeds.across_back((far_column,))
        early_columns = earlies.across_back((jnp.concatenate(earlies.columns, axis=0),))
        small.step()
        links.slot((lates.got, feeds.got, small.rows))
        late_columns = lates.across_back()
        feeds.core_back(
            tuple(column for pair in zip(near_columns, far_columns) for column in pair)
        )
        small.step()
        small.step()
        square = (
            shaped((width, units), jnp.float32),
            shaped((units, width), jnp.float32),
        )
        down_grad, out_grad, up_grad = place_pieces(
            finish_feed_kernel,
            "feed_places",
            places,
            (feeds.result,),
            (square[1], square[1], square[0]),
        )
        links.slot((lates.got, small.rows, up_grad))
        lates.core_back(late_columns)
        earlies.core_back(early_columns)
        small.step()
        rowwise = small.rows
        attend_matrix_grads = place_pieces(
            finish_kernel,
            "attend_places",
            places,
            ((earlies.result, lates.result),),
            (square[0],) * 3,
        )
    else:
        widths = (units, width - units)
        step = back(live, 0, widths, (), ())
        latents_gradient = latents_step(live, step[0], 0, crops, ())
        together = lambda own, rest: jnp.roll(
            jnp.concatenate([own, rest]).reshape(narrow, units), place, axis=0
        ).reshape(-1)
        shift_grad = step[4].sum(axis=0)
        rows = jnp.stack(
            [
                (step[3].sum(axis=1) - first_shift * shift_grad) / first_gain,
                shift_grad,
                *(feed_vectors[row] for row in range(4)),
                together(step[2][0][0], step[2][1][0]),
                together(step[2][0][2], step[2][1][2]),
                together(up_bias_grads[0][0], up_bias_grads[1][0]),
            ]
        )
        rowwise = lax.psum(rows, ("wide", "narrow"))
        joined = step[1][0]
        attend_matrix_grads = tuple(
            links.reduce_plain(
                joined[:, kind * units : (kind + 1) * units],
                lax.slice_in_dim(
                    joined,
                    3 * units + kind * widths[1],
                    3 * units + (kind + 1) * widths[1],
                    axis=1,
                ),
                1,
            )
            for kind in range(3)
        )
        down_grad, out_grad, up_grad = (
            links.reduce_plain(*grads, axis) for grads, axis in zip(feed_packed, (0, 0, 1))
        )
    own = lax.dynamic_slice_in_dim(rowwise[6:9], place * units, units, 1)
    return (
        block_output,
        latents_gradient,
        *attend_matrix_grads,
        out_grad,
        up_grad,
        down_grad,
        own[0],
        own[1],
        own[2],
        rowwise[4],
        rowwise[5],
        rowwise[0],
        rowwise[1],
        rowwise[2],
        rowwise[3],
    )


def solution(mesh):
    rows = P(("wide", "narrow"), None)
    columns = P(None, "narrow")
    units = P("narrow", None)
    vector = P("narrow")
    whole = P()
    return jax.shard_map(
        on_device,
        mesh=mesh,
        in_specs=(
            rows,
            rows,
            whole,
            whole,
            columns,
            columns,
            columns,
            units,
            columns,
            units,
            vector,
            vector,
            vector,
            whole,
            whole,
            whole,
            whole,
            whole,
            whole,
        ),
        out_specs=(
            rows,
            rows,
            columns,
            columns,
            columns,
            units,
            columns,
            units,
            vector,
            vector,
            vector,
            whole,
            whole,
            whole,
            whole,
            whole,
            whole,
        ),
        check_vma=False,
    )
```

```python
from functools import partial
import math

import jax
import jax.numpy as jnp
from jax import lax
from jax.experimental import pallas as pl
from jax.experimental.pallas import tpu as pltpu
from jax.sharding import PartitionSpec as P

HS = 128
CROP = 512


EPSILON = 1e-05


def dot(left, right, left_dim, right_dim):
    return lax.dot_general(
        left,
        right,
        (((left_dim,), (right_dim,)), ((), ())),
        preferred_element_type=jnp.float32,
    )


def unit_rows(rows):
    center = rows - jnp.mean(rows, axis=-1, keepdims=True)
    inverse = lax.rsqrt(jnp.mean(center * center, axis=-1, keepdims=True) + EPSILON)
    return center * inverse, inverse


def unit_rows_back(scaled, unit, inverse):
    inner = scaled - jnp.mean(scaled, axis=-1, keepdims=True)
    return (inner - unit * jnp.mean(scaled * unit, axis=-1, keepdims=True)) * inverse


def low(array):
    return array.astype(jnp.bfloat16)


def attend_kernel(first, start, carried, live_ref, source_ref, *refs):
    if first:
        gain_ref, shift_ref, *refs = refs
    query_weight, key_weight, value_weight, query_bias, value_bias, *refs = refs
    refs = refs[carried:]
    if first:
        normed_ref, *refs = refs
    query_ref, keys_ref, values_ref, weights_ref, attended_ref, inverse_ref = refs

    @pl.when(pl.program_id(0) + start < live_ref[0])
    def _():
        if first:
            unit, _ = unit_rows(source_ref[...].astype(jnp.float32))
            normed_ref[...] = low(unit * gain_ref[...] + shift_ref[...])
            normed = normed_ref[...]
        else:
            normed = source_ref[...]
        query_ref[...] = low(dot(normed, query_weight[...], 1, 0) + query_bias[...])
        keys_ref[...] = low(dot(normed, key_weight[...], 1, 0))
        values_ref[...] = low(dot(normed, value_weight[...], 1, 0) + value_bias[...])
        ones = jnp.ones((CROP, HS), jnp.bfloat16)
        for head in range(query_ref.shape[1] // HS):
            columns = pl.ds(head * HS, HS)
            scores = dot(query_ref[:, columns], keys_ref[:, columns], 1, 1)
            highest = jnp.max(scores, axis=-1, keepdims=True)
            weights = low(jnp.exp2((scores - highest) * (math.log2(math.e) / math.sqrt(HS))))
            weights_ref[head] = weights
            extended = jnp.concatenate([values_ref[:, columns], ones], axis=1)
            mixed = dot(weights, extended, 1, 0)
            inverse = 1.0 / mixed[:, HS:]
            inverse_ref[:, columns] = inverse
            attended_ref[:, columns] = low(mixed[:, :HS] * inverse)


def cut_kernel(places_ref, cuts, extra, *outputs):
    for pieces, target in zip(cuts, outputs):
        row = 0
        width = target.shape[1]
        for piece in pieces:
            rows = piece.shape[0]
            for side in range(piece.shape[1] // width):
                target[row : row + rows, :] = piece[:, side * width : (side + 1) * width]
                row += rows
    if extra:
        rows = [array[...].astype(jnp.float32).reshape(1, -1) for array in extra]
        rows += [jnp.zeros_like(rows[0])] * (EXTRA - len(rows))
        outputs[0][outputs[0].shape[0] - EXTRA :] = low(jnp.concatenate(rows, axis=0))


def fill_kernel(firsts, places_ref, near, far, *outputs):
    for pieces, core in ((near, places_ref[0]), (far, 1 - places_ref[0])):
        starts = (places_ref[1], 1 - places_ref[1], 1)
        for source, start, eighths, row in zip(pieces, starts, (1, 1, 2), firsts):
            width = source.shape[1]
            for output in outputs:
                size = output.shape[0] * eighths // 8
                base = core * (output.shape[0] // 2) + start * size
                rows = pl.ds(pl.multiple_of(base, size), size)
                for side in range(output.shape[1] // width):
                    output[rows, side * width : (side + 1) * width] = source[row : row + size, :]
                    row += size


EXTRA = 16


def gelu_pair(before):
    lower = 0.5 + 0.5 * lax.erf(before * math.sqrt(0.5))
    density = jnp.exp2(before * before * (-0.5 * math.log2(math.e)))
    slope = lower + before * density * (1.0 / math.sqrt(2.0 * math.pi))
    return before * lower, slope


def feed_kernel(
    crops,
    split,
    live_ref,
    latents_ref,
    cotangent_ref,
    attended_refs,
    out_weights,
    up_weights,
    down_weights,
    up_biases,
    out_bias,
    down_bias,
    gain,
    shift,
    output_ref,
    hidden_grad_ref,
    attended_grads,
    packed,
    up_bias_grads,
    vectors_ref,
    out_sums,
    up_sums,
    down_sums,
):
    step = pl.program_id(0)

    @pl.when(step == 0)
    def _():
        for sums in (*out_sums, *up_sums, *down_sums, *up_bias_grads, vectors_ref):
            sums[...] = jnp.zeros_like(sums)

    @pl.when(step >= live_ref[0])
    def _():
        output_ref[...] = jnp.zeros_like(output_ref)
        hidden_grad_ref[...] = jnp.zeros_like(hidden_grad_ref)

    @pl.when(step < live_ref[0])
    def _():
        hidden = latents_ref[...].astype(jnp.float32) + out_bias[...]
        for part in range(2):
            hidden = hidden + dot(attended_refs[part][...], out_weights[part][...], 1, 0)
        unit, inverse = unit_rows(hidden)
        normed = low(unit * gain[...] + shift[...])
        top = cotangent_ref[...]
        result = hidden + down_bias[...]
        second_grad = jnp.zeros(hidden.shape, jnp.float32)
        for part in range(2):
            before = dot(normed, up_weights[part][...], 1, 0) + up_biases[part][...]
            value, slope = gelu_pair(before)
            activated = low(value)
            result = result + dot(activated, down_weights[part][...], 1, 0)
            down_sums[part][...] += dot(activated, top, 0, 0)
            activated_grad = dot(top, down_weights[part][...], 1, 1)
            before_grad = low(activated_grad * slope)
            up_bias_grads[part][...] += jnp.sum(
                before_grad.astype(jnp.float32), axis=0, keepdims=True
            )
            up_sums[part][...] += dot(normed, before_grad, 0, 0)
            second_grad = second_grad + dot(before_grad, up_weights[part][...], 1, 1)
        output_ref[...] = low(result)
        top_grad = top.astype(jnp.float32)
        hidden_grad = top_grad + unit_rows_back(second_grad * gain[...], unit, inverse)
        hidden_grad_ref[...] = hidden_grad
        hidden_low = low(hidden_grad)
        for part in range(2):
            out_sums[part][...] += dot(attended_refs[part][...], hidden_low, 0, 0)
            attended_grads[part][...] = low(dot(hidden_low, out_weights[part][...], 1, 1))
        for row, term in enumerate((second_grad * unit, second_grad, hidden_grad, top_grad)):
            vectors_ref[row : row + 1] += jnp.sum(term, axis=0, keepdims=True)

    @pl.when(step == crops - 1)
    def _():
        if not split:
            for grads, sums in zip(packed, (down_sums, out_sums, up_sums)):
                for part in range(2):
                    grads[part][...] = low(sums[part][...])
            return
        for group, core in zip(packed, (live_ref[1], 1 - live_ref[1])):
            tall_ref, flat_ref = group
            rows = flat_ref.shape[0] // 2
            short = tall_ref.shape[0] // (4 * PIECES)
            half = tall_ref.shape[1] // 2
            for part in range(2):
                flat_ref[part * rows : (part + 1) * rows] = low(
                    up_sums[part][pl.ds(pl.multiple_of(core * rows, rows), rows), :]
                )
                for piece in range(PIECES):
                    start = core * (PIECES * short) + piece * short
                    source = pl.ds(pl.multiple_of(start, short), short)
                    for side in range(2):
                        base = part * rows + (2 * piece + side) * short
                        across = pl.ds(side * half, half)
                        for index, sums in enumerate((down_sums, out_sums)):
                            tall_ref[base : base + short, index * half : (index + 1) * half] = low(
                                sums[part][source, across]
                            )


def attend_back_kernel(
    crops,
    split,
    live_ref,
    normed_ref,
    queries,
    keys,
    values,
    weights,
    inverses,
    attended,
    attended_grads,
    matrices,
    previous,
    packed_before,
    grads,
    packed,
    bias_grads,
    gain_terms,
    shift_terms,
    joined,
    sums,
):
    step = pl.program_id(0)
    scale = 1.0 / math.sqrt(HS)
    widths = [ref.shape[1] for ref in queries]
    bases = (0, 3 * widths[0])

    @pl.when(step == 0)
    def _():
        sums[...] = jnp.zeros_like(sums)
        for part in range(2):
            bias_grads[part][...] = jnp.zeros_like(bias_grads[part])

    @pl.when(step < live_ref[0])
    def _():
        for part in range(2):
            for head in range(widths[part] // HS):
                columns = pl.ds(head * HS, HS)

                def put(kind, value):
                    value = low(value)
                    grads[kind][part][:, columns] = value
                    joined[:, pl.ds(bases[part] + kind * widths[part] + head * HS, HS)] = value

                inner = attended_grads[part][:, columns].astype(jnp.float32)
                inner = inner * inverses[part][:, columns]
                upstream = low(inner)
                total = jnp.sum(
                    inner * attended[part][:, columns].astype(jnp.float32), axis=1, keepdims=True
                )
                head_weights = weights[part][head]
                put(2, dot(head_weights, upstream, 0, 0))
                probs_grad = dot(upstream, values[part][:, columns], 1, 1)
                scores_grad = low(head_weights.astype(jnp.float32) * (probs_grad - total))
                put(0, dot(scores_grad, keys[part][:, columns], 1, 0) * scale)
                put(1, dot(scores_grad, queries[part][:, columns], 0, 0) * scale)
            for kind in range(3):
                bias_grads[part][kind : kind + 1] += jnp.sum(
                    grads[kind][part][...].astype(jnp.float32), axis=0, keepdims=True
                )
        sums[...] += dot(normed_ref[...], joined[...], 0, 0)

    @pl.when(step == crops - 1)
    def _():
        gain_terms[...] = jnp.zeros_like(gain_terms)
        shift_terms[...] = jnp.zeros_like(shift_terms)
        for part in range(2):
            for kind in range(3):
                matrix = matrices[kind][part]
                base = bases[part] + kind * widths[part]
                for start in range(0, widths[part], HS):
                    gain_terms[...] += sums[:, pl.ds(base + start, HS)] * matrix[
                        :, pl.ds(start, HS)
                    ].astype(jnp.float32)
                bias = bias_grads[part][kind : kind + 1]
                rough = low(bias)
                fine = low(bias - rough.astype(jnp.float32))
                shift_terms[...] += dot(
                    jnp.concatenate([rough, fine] + [jnp.zeros_like(rough)] * 6, axis=0),
                    matrix[...],
                    1,
                    1,
                )
        if not split:
            packed[0][...] = low(sums[...])
            return
        half = sums.shape[0] // 2
        for target, core in zip(packed, (live_ref[1], 1 - live_ref[1])):
            rows = pl.ds(pl.multiple_of(core * half, half), half)
            for part in range(2):
                target[part * half : (part + 1) * half] = low(
                    sums[rows, pl.ds(bases[part], 3 * widths[part])]
                )


def latents_kernel(
    first, live_ref, latents_ref, hidden_grad_ref, grads, matrices, gain_ref, previous, output_ref
):
    crop = pl.program_id(0) + first

    @pl.when(crop >= live_ref[0])
    def _():
        output_ref[...] = jnp.zeros_like(output_ref)

    @pl.when(crop < live_ref[0])
    def _():
        unit, inverse = unit_rows(latents_ref[...].astype(jnp.float32))
        upstream = jnp.zeros(output_ref.shape, jnp.float32)
        for kind in range(3):
            for grad, matrix in zip(grads[kind], matrices[kind]):
                upstream = upstream + dot(grad[...], matrix[...], 1, 1)
        output_ref[...] = hidden_grad_ref[...] + unit_rows_back(
            upstream * gain_ref[...], unit, inverse
        )


def finish_kernel(places_ref, groups, *outputs):
    for half, group in enumerate(groups):
        for index, source in enumerate(group):
            pieces = 16 // len(group)
            size = source.shape[0] // pieces
            width = source.shape[1] // 6
            for piece in range(pieces):
                start = pl.multiple_of(places_ref[index * pieces + piece] * size, size)
                for column in range(6):
                    phase, kind = 2 * half + column // 3, column % 3
                    outputs[kind][pl.ds(start, size), pl.ds(phase * width, width)] = source[
                        piece * size : (piece + 1) * size, pl.ds(column * width, width)
                    ].astype(jnp.float32)


def finish_feed_kernel(places_ref, sources, down_ref, out_ref, up_ref):
    half = up_ref.shape[1]
    for index, source in enumerate(sources):
        pieces = 16 // len(sources)
        size = source.shape[0] // pieces
        short = size // 2
        for piece in range(pieces):
            place = places_ref[index * pieces + piece]
            up_ref[pl.ds(pl.multiple_of(place * size, size), size), :] = source[
                piece * size : (piece + 1) * size, pl.ds(2 * half, half)
            ].astype(jnp.float32)
            rows = pl.ds(pl.multiple_of(place * short, short), short)
            for side in range(2):
                start = piece * size + side * short
                for column, target in enumerate((down_ref, out_ref)):
                    target[rows, pl.ds(side * half, half)] = source[
                        start : start + short, pl.ds(column * half, half)
                    ].astype(jnp.float32)


def rows_kernel(
    place_ref, gains, shifts, biases, feed_vectors, up_biases, gain_ref, shift_ref, rows_ref
):
    gain_terms = gains[0][...]
    shift_terms = shifts[0][...]
    for more in gains[1:]:
        gain_terms = gain_terms + more[...]
    for more in shifts[1:]:
        shift_terms = shift_terms + more[...]
    shift_grad = jnp.sum(shift_terms, axis=0, keepdims=True)
    unscaled = jnp.sum(gain_terms.T, axis=0, keepdims=True)
    rows_ref[...] = jnp.zeros_like(rows_ref)
    rows_ref[0:1] = (unscaled - shift_ref[...] * shift_grad) / gain_ref[...]
    rows_ref[1:2] = shift_grad
    rows_ref[2:6] = feed_vectors[0:4]

    def put(row, own, rest):
        own = jnp.concatenate(own, axis=1)
        rest = jnp.concatenate(rest, axis=1)
        rows_ref[row : row + 1] = jnp.where(
            place_ref[0] == 0,
            jnp.concatenate([own, rest], axis=1),
            jnp.concatenate([rest, own], axis=1),
        )

    for row, kind in ((6, 0), (7, 2)):
        put(row, *([pair[part][kind : kind + 1] for pair in biases] for part in range(2)))
    put(8, *([array[...]] for array in up_biases))


PIECES = 8
VMEM_LIMIT = 66_000_000
COST_SCALE = 8


def row_block(width, column=0):
    return pl.BlockSpec((CROP, width), lambda i, live: (i, column))


def fixed(rows, width, column=0):
    return pl.BlockSpec((rows, width), lambda i, live: (0, column), pipeline_mode=pl.Buffered(1))


def shaped(shape, dtype=jnp.bfloat16):
    return jax.ShapeDtypeStruct(shape, dtype)


def run(
    kernel, name, crops, in_specs, out_specs, out_shape, flops, moved, scratch=(), aliases=None
):
    return pl.pallas_call(
        kernel,
        input_output_aliases=aliases or {},
        name=name,
        out_shape=out_shape,
        grid_spec=pltpu.PrefetchScalarGridSpec(
            num_scalar_prefetch=1,
            grid=(crops,),
            in_specs=in_specs,
            out_specs=out_specs,
            scratch_shapes=scratch,
        ),
        compiler_params=pltpu.CompilerParams(
            dimension_semantics=("arbitrary",), vmem_limit_bytes=VMEM_LIMIT
        ),
        cost_estimate=pl.CostEstimate(
            flops=COST_SCALE * flops, bytes_accessed=COST_SCALE * moved, transcendentals=0
        ),
    )


def attend(live, source, norm, matrices, biases, start, size, previous=()):
    count, width = source.shape
    crops = count // CROP
    units = matrices[0].shape[1]
    heads = units // HS
    first = norm is not None
    vector = fixed(1, units)
    block = lambda width: pl.BlockSpec((CROP, width), lambda i, live: (i + start, 0))
    outs = (block(width),) * first + (
        block(units),
        block(units),
        block(units),
        pl.BlockSpec((None, heads, CROP, CROP), lambda i, live: (i + start, 0, 0, 0)),
        block(units),
        block(units),
    )
    rows = shaped((count, units))
    shapes = (shaped((count, width)),) * first + (
        rows,
        rows,
        rows,
        shaped((crops, heads, CROP, CROP)),
        rows,
        shaped((count, units), jnp.float32),
    )
    operands = (live, source, *(norm or ()), *matrices, *biases)
    done = size * CROP
    return run(
        partial(attend_kernel, first, start, len(previous)),
        "attend_first" if first else "attend_rest",
        size,
        (block(width),)
        + (fixed(1, width),) * (2 * first)
        + (fixed(width, units),) * 3
        + (vector,) * 2
        + (pl.BlockSpec(memory_space=pl.ANY),) * len(previous),
        outs,
        shapes,
        2 * done * units * (3 * width + 2 * CROP),
        done * (units * (12 + 2 * CROP // HS) + 4 * width),
        (),
        {len(operands) + i: i for i in range(len(previous))},
    )(*operands, *previous)


def feed(live, latents, cotangent, attended, outs, ups, downs, up_biases, vectors, split):
    count, width = latents.shape
    crops = count // CROP
    units = [array.shape[1] for array in attended]
    both = lambda make: tuple(make(size) for size in units)
    row_in = both(row_block)
    tall = both(lambda size: fixed(size, width))
    flat = both(lambda size: fixed(width, size))
    thin = both(lambda size: fixed(1, size))
    vector = fixed(1, width)
    sums = lambda dtype: (
        both(lambda size: dtype((size, width))),
        both(lambda size: dtype((width, size))),
        both(lambda size: dtype((size, width))),
    )
    if split:
        packed_specs = ((fixed(width, width), fixed(width, width // 2)),) * 2
        packed_shapes = ((shaped((width, width)), shaped((width, width // 2))),) * 2
    else:
        packed_specs = (tall, tall, flat)
        out_shapes, up_shapes, down_shapes = sums(shaped)
        packed_shapes = (down_shapes, out_shapes, up_shapes)
    return run(
        partial(feed_kernel, crops, split),
        "feed",
        crops,
        (row_block(width), row_block(width), row_in, tall, flat, tall, thin)
        + (vector,) * 4,
        (row_block(width), row_block(width), row_in, packed_specs, thin, fixed(8, width)),
        (
            shaped((count, width)),
            shaped((count, width), jnp.float32),
            both(lambda size: shaped((count, size))),
            packed_shapes,
            both(lambda size: shaped((1, size), jnp.float32)),
            shaped((8, width), jnp.float32),
        ),
        2 * count * width * width * 9,
        count * width * 14,
        sums(lambda shape: pltpu.VMEM(shape, jnp.float32)),
    )(live, latents, cotangent, attended, outs, ups, downs, up_biases, *vectors)


def attend_back(
    live, normed, saved, attended_grads, matrices, widths, phase, previous, packed_before, split
):
    count, width = normed.shape
    crops = count // CROP
    both = lambda make: tuple(make(size) for size in widths)
    units = [array.shape[1] for array in saved[0]]
    rows = both(lambda size: row_block(size, phase))
    heads = both(
        lambda size: pl.BlockSpec(
            (None, size // HS, CROP, CROP), lambda i, live: (i, phase, 0, 0)
        )
    )
    flat = both(lambda size: fixed(width, size, phase))
    queries, keys, values, weights, attended, inverses = saved
    joined = 3 * sum(widths)
    if split:
        packed_specs = (fixed(width, joined // 2, phase % 2),) * 2
        packed_shapes = (shaped((width, joined)),) * 2
    else:
        packed_specs = (fixed(width, joined),)
        packed_shapes = (shaped((width, joined)),)
    operands = (
        live,
        normed,
        queries,
        keys,
        values,
        weights,
        inverses,
        attended,
        attended_grads,
        matrices,
    )
    before = len(jax.tree.leaves(operands))
    carried = len(jax.tree.leaves(previous))
    aliases = {before + i: i for i in range(carried)}
    for i in range(len(packed_before)):
        aliases[before + carried + i] = 6 + i
    untouched = lambda arrays: jax.tree.map(lambda _: pl.BlockSpec(memory_space=pl.ANY), arrays)
    return run(
        partial(attend_back_kernel, crops, split),
        "attend_back",
        crops,
        (row_block(width), rows, rows, rows, heads, rows, rows, rows, (flat,) * 3)
        + (untouched(previous), untouched(packed_before)),
        (
            (rows,) * 3,
            packed_specs,
            both(lambda size: fixed(8, size)),
            fixed(width, HS),
            fixed(8, width),
        ),
        (
            (tuple(shaped((count, size)) for size in units),) * 3,
            packed_shapes,
            both(lambda size: shaped((8, size), jnp.float32)),
            shaped((width, HS), jnp.float32),
            shaped((8, width), jnp.float32),
        ),
        2 * count * sum(widths) * (3 * width + 4 * CROP),
        count * (sum(widths) * (18 + 2 * CROP // HS) + 2 * width),
        (
            pltpu.VMEM((CROP, joined), jnp.bfloat16),
            pltpu.VMEM((width, joined), jnp.float32),
        ),
        aliases,
    )(*operands, previous, packed_before)


def latents_back(live, latents, hidden_grad, grads, matrices, gain, first, crops, previous):
    count, width = latents.shape
    block = lambda size: pl.BlockSpec((CROP, size), lambda i, live: (i + first, 0))
    rows = tuple(tuple(block(array.shape[1]) for array in kind) for kind in grads)
    flat = tuple(tuple(fixed(*array.shape) for array in kind) for kind in matrices)
    operands = (live, latents, hidden_grad, grads, matrices, gain)
    before = len(jax.tree.leaves(operands))
    return run(
        partial(latents_kernel, first),
        "latents_back",
        crops,
        (block(width), block(width), rows, flat, fixed(1, width))
        + (tuple(pl.BlockSpec(memory_space=pl.ANY) for _ in previous),),
        block(width),
        shaped((count, width), jnp.float32),
        2 * crops * CROP * width * width * 3,
        crops * CROP * width * 16,
        (),
        {before + i: i for i in range(len(previous))},
    )(*operands, previous)


def place_pieces(kernel, name, places, operands, out_shape):
    return pl.pallas_call(
        kernel,
        name=name,
        out_shape=out_shape,
        grid_spec=pltpu.PrefetchScalarGridSpec(
            num_scalar_prefetch=1,
            grid=(1,),
            in_specs=jax.tree.map(
                lambda array: pl.BlockSpec(array.shape, lambda i, places: (0, 0)), operands
            ),
            out_specs=jax.tree.map(
                lambda array: pl.BlockSpec(array.shape, lambda i, places: (0, 0)), out_shape
            ),
        ),
        compiler_params=pltpu.CompilerParams(
            dimension_semantics=("arbitrary",), vmem_limit_bytes=VMEM_LIMIT
        ),
    )(places, *operands)


def cut_weights(places, weights, cuts, extra=()):
    width = min(weight.shape[1] for weight in weights)
    eighth = lambda i, places: (places[0] * 4 + places[1], 0)
    quarter = lambda i, places: (places[0] * 2 + 1, 0)
    specs = tuple(
        tuple(
            pl.BlockSpec(
                (weights[k].shape[0] // (8 if shared else 4), weights[k].shape[1]),
                eighth if shared else quarter,
            )
            for k, shared in cut
        )
        for cut in cuts
    )
    rows = [sum(weights[k].size // (8 if shared else 4) for k, shared in cut) // width for cut in cuts]
    if extra:
        rows[0] += EXTRA
    shapes = tuple(shaped((count, width)) for count in rows)
    whole = lambda array: pl.BlockSpec(array.shape, lambda i, places: (0,) * len(array.shape))
    return pl.pallas_call(
        cut_kernel,
        name="cut_weights",
        out_shape=shapes,
        grid_spec=pltpu.PrefetchScalarGridSpec(
            num_scalar_prefetch=1,
            grid=(1,),
            in_specs=(specs, tuple(whole(array) for array in extra)),
            out_specs=tuple(whole(shape) for shape in shapes),
        ),
        compiler_params=pltpu.CompilerParams(
            dimension_semantics=("arbitrary",), vmem_limit_bytes=VMEM_LIMIT
        ),
    )(places, tuple(tuple(weights[k] for k, _ in cut) for cut in cuts), extra)


def pair_perm(size, bit):
    return [(i, i ^ bit) for i in range(size)]


def after(value, *needed):
    return lax.optimization_barrier((value, needed))[0]


class Links:
    def __init__(self):
        self.wide = lax.axis_size("wide")
        self.narrow = lax.axis_size("narrow")
        self.paired = self.narrow == 2 and self.wide == 16
        self.index = lax.axis_index("wide")
        self.core = self.index % 2
        self.across = (self.index // 2) % 2
        self.along = self.index // 4
        self.token = ()
        self.sent = ()

    def slot(self, token):
        self.token = token
        self.sent = ()

    def swap(self, array, bit):
        return lax.ppermute(array, "wide", pair_perm(self.wide, bit))

    def swap_narrow(self, array):
        return lax.ppermute(array, "narrow", [(0, 1), (1, 0)])

    def others(self, weight, axis):
        whole = lax.all_gather(weight, "narrow", axis=0, tiled=False)
        whole = jnp.roll(whole, -lax.axis_index("narrow"), axis=0)[1:]
        return jnp.concatenate([whole[i] for i in range(self.narrow - 1)], axis=axis)

    def places(self):
        return jnp.stack(
            [
                (self.core ^ core) * 8 + (self.across ^ across) * 4 + (self.along ^ along)
                for core in range(2)
                for across in range(2)
                for along in (0, 2, 1, 3)
            ]
        ).astype(jnp.int32)

    def reduce_plain(self, own, other, axis):
        width = own.shape[axis]
        parts = jnp.stack(
            [own]
            + [
                lax.slice_in_dim(other, i * width, (i + 1) * width, axis=axis)
                for i in range(self.narrow - 1)
            ]
        )
        parts = jnp.roll(parts, lax.axis_index("narrow"), axis=0)
        mine = lax.psum_scatter(parts, "narrow", scatter_dimension=0, tiled=True)[0]
        return lax.psum(mine, "wide").astype(jnp.float32)


def total(terms, size):
    parts = [
        lax.dynamic_slice_in_dim(array, start, size, 0).astype(jnp.float32)
        for array, start in terms
    ]
    return sum(parts[1:], parts[0]).astype(jnp.bfloat16)


def moved(terms, rows):
    return [(array, start + rows) for array, start in terms]


class Exchange:
    def __init__(self, links):
        self.links = links

    def waiting(self, terms):
        return [(after(array, self.links.token), start) for array, start in terms]

    def exchange(self, arrays, *sends):
        arrays = tuple(after(array, self.links.token) for array in arrays)
        self.links.sent += arrays
        return tuple(send(array) for send, array in zip(sends, arrays))


class Reduction(Exchange):
    def __init__(self, links, keep, give):
        super().__init__(links)
        self.rows = keep.shape[0] // 2
        self.own = [(keep, 0)]
        self.other = [(keep, self.rows)]
        self.give = give

    def cores(self):
        (got,) = self.exchange([self.give], lambda array: self.links.swap(array, 1))
        self.own += [(got, 0)]
        self.other += [(got, self.rows)]

    def narrows(self):
        give = total(self.waiting(self.other), self.rows)
        (got,) = self.exchange([give], self.links.swap_narrow)
        self.own += [(got, 0)]
        self.other = []
        self.got = got

    def acrosses(self):
        size = self.rows // 2
        across = self.links.across
        parts = [self.waiting(terms) for terms in (self.own, self.other) if terms]
        gives = [total(moved(terms, (1 - across) * size), size) for terms in parts]
        give = jnp.concatenate(gives, axis=0) if len(gives) > 1 else gives[0]
        (got,) = self.exchange([give], lambda array: self.links.swap(array, 2))
        self.own = moved(self.own, across * size) + [(got, 0)]
        if self.other:
            self.other = moved(self.other, across * size) + [(got, size)]
        self.rows = size
        self.got = got


class Ending(Exchange):
    def __init__(self, links, groups):
        super().__init__(links)
        self.groups = groups
        self.swaps = [
            lambda array: links.swap(array, 4),
            lambda array: links.swap(array, 8),
            lambda array: links.swap(array, 12),
        ]

    def alongs(self):
        size = self.groups[0].rows // 4
        for group in self.groups:
            group.own = self.waiting(group.own)
        terms = lambda group, bit: moved(group.own, (self.links.along ^ bit) * size)
        gives = [
            jnp.concatenate([total(terms(group, bit), size) for group in self.groups], axis=1)
            for bit in range(1, 4)
        ]
        got = self.exchange(gives, *self.swaps)
        self.parts = [terms(group, 0) for group in self.groups]
        self.size = size
        self.got = got

    def piece(self):
        got = [after(array, self.links.token) for array in self.got]
        pieces = []
        column = 0
        for terms in self.parts:
            width = terms[0][0].shape[1]
            mine = [
                (lax.slice_in_dim(array, column, column + width, axis=1), 0) for array in got
            ]
            pieces.append(total(self.waiting(terms) + mine, self.size))
            column += width
        return jnp.concatenate(pieces, axis=1)

    def along_back(self):
        piece = self.piece()
        self.got = self.exchange([piece] * 3, *self.swaps)
        near, far, opposite = self.got
        self.column = (piece, far, near, opposite)

    def far_back(self):
        piece = self.piece()
        self.got = self.exchange([piece], self.swaps[1])
        self.column = (piece, *self.got)

    def near_back(self):
        column = self.whole_column()
        self.got = self.exchange([column], self.swaps[0])
        self.columns = (column, *self.got)

    def whole_column(self):
        return jnp.concatenate([after(array, self.links.token) for array in self.column], axis=0)

    def across_back(self, columns=None):
        columns = columns or (self.whole_column(),)
        self.got = self.exchange(columns, *(len(columns) * (lambda array: self.links.swap(array, 2),)))
        return (*columns, *self.got)

    def core_back(self, columns):
        swap = lambda array: self.links.swap(array, 1)
        got = self.exchange(columns, *(len(columns) * (swap,)))
        self.result = (*columns, *got)


class SmallSum(Exchange):
    def __init__(self, links, rows):
        super().__init__(links)
        self.rows = rows
        self.left = [
            lambda rows: links.swap(rows, 2),
            lambda rows: links.swap(rows, 1),
            links.swap_narrow,
            lambda rows: links.swap(rows, 4),
            lambda rows: links.swap(rows, 8),
        ]

    def step(self):
        (got,) = self.exchange([self.rows], self.left.pop(0))
        self.rows = self.rows + got


def on_device(
    latents,
    cotangent,
    crop_counts,
    image_device,
    query_weight,
    key_weight,
    value_weight,
    out_weight,
    up_weight,
    down_weight,
    query_bias,
    value_bias,
    up_bias,
    out_bias,
    down_bias,
    first_gain,
    first_shift,
    second_gain,
    second_shift,
):
    links = Links()
    paired = links.paired
    count = latents.shape[0]
    crops = count // CROP
    width = latents.shape[1]
    narrow = links.narrow
    place = lax.axis_index("narrow")
    owned = jnp.sum(jnp.where(image_device == lax.axis_index("wide"), crop_counts, 0))
    live = jnp.stack([owned - place * crops, links.core]).astype(jnp.int32)
    units = query_weight.shape[1]
    vector = lambda array: array.reshape(1, -1)
    own_biases = jnp.stack([query_bias, value_bias, up_bias])
    rows_of = lambda array: tuple(array[i : i + 1].astype(jnp.float32) for i in range(3))
    norm = (vector(first_gain), vector(first_shift))
    own_weights = (query_weight, key_weight, value_weight)
    feed_weights = (out_weight, down_weight, up_weight)
    first_step = lambda live, start, size, previous: attend(
        live, latents, norm, own_weights, rows_of(own_biases)[:2], start, size, previous
    )
    rest_step = lambda live: attend(
        live, first, None, rest_weights, rows_of(rest_biases)[:2], 0, crops
    )
    if paired:
        spots = jnp.stack([links.core, links.across]).astype(jnp.int32)
        unfilled = lambda weights: tuple(shaped(weight.shape) for weight in weights)
        cores = lambda pieces: tuple(links.swap(piece, 1) for piece in pieces)
        begin = crops // 2
        part = lambda numbers, shared: tuple((k, shared) for k in numbers)
        cuts = cut_weights(
            spots,
            own_weights + feed_weights,
            (part(range(3), True), part(range(3), False) + part(range(3, 6), True)),
            (query_bias, value_bias, up_bias),
        )
        shared, direct = (links.swap_narrow(cut) for cut in cuts)
        early = first_step(after(live, cuts), 0, begin, ())
        shared = after(shared, early[0])
        (feed_cut,) = cut_weights(
            after(spots, early[0]), feed_weights, (part(range(3), False),)
        )
        first, *saved_own = first_step(
            after(live, (shared, feed_cut)), begin, crops - begin, tuple(early)
        )
        feed_direct = links.swap_narrow(feed_cut)
        relayed = links.swap(shared, 2)
        rest_biases = shared[shared.shape[0] - EXTRA :]
        pieces = after((shared, relayed, direct), (first, feed_cut))
        far = cores(pieces)
        rest_weights = place_pieces(
            partial(fill_kernel, (0, 0, 0)),
            "fill_attend",
            spots,
            (pieces, far),
            unfilled(own_weights),
        )
        rows = sum(weight.shape[0] // 4 for weight in own_weights)
        feed_shared = pieces[2][rows:]
        feed_relayed = links.swap(feed_shared, 2)
        saved_rest = rest_step(after(live, feed_shared))
        later = after((feed_relayed, feed_direct), saved_rest[0])
        later_far = cores(later)
        rest_out, rest_down, rest_up = place_pieces(
            partial(fill_kernel, (rows, 0, 0)),
            "fill_feed",
            spots,
            ((pieces[2], *later), (far[2], *later_far)),
            unfilled(feed_weights),
        )
    else:
        first, *saved_own = first_step(live, 0, crops, ())
        rest_biases = lax.all_gather(own_biases, "narrow", axis=0)
        rest_biases = jnp.roll(rest_biases, -place, axis=0).transpose(1, 0, 2).reshape(3, -1)
        rest_biases = rest_biases[:, units:]
        rest_weights = tuple(links.others(weight, 1) for weight in own_weights)
        saved_rest = rest_step(live)
        rest_out = links.others(out_weight, 0)
        rest_up = links.others(up_weight, 1)
        rest_down = links.others(down_weight, 0)
    up_biases = (rows_of(own_biases)[2], rows_of(rest_biases)[2])
    matrices = tuple(zip(own_weights, rest_weights))
    outs = (out_weight, rest_out)
    ups = (up_weight, rest_up)
    downs = (down_weight, rest_down)
    saved = tuple(zip(saved_own, saved_rest))
    (
        block_output,
        hidden_grad,
        attended_grads,
        feed_packed,
        up_bias_grads,
        feed_vectors,
    ) = feed(
        live,
        latents,
        cotangent,
        saved[4],
        outs,
        ups,
        downs,
        up_biases,
        [vector(array) for array in (out_bias, down_bias, second_gain, second_shift)],
        paired,
    )

    def back(live, phase, widths, previous, packed_before):
        return attend_back(
            live,
            first,
            saved,
            attended_grads,
            matrices,
            widths,
            phase,
            previous,
            packed_before,
            paired,
        )

    def latents_step(live, grads, start, size, previous):
        return latents_back(
            live, latents, hidden_grad, grads, matrices, norm[0], start, size, previous
        )

    if paired:
        phases = units // HS
        widths = (HS, (width - units) // phases)
        ready = lambda: after(live, links.sent)
        tall, flat = (Reduction(links, keep, give) for keep, give in zip(*feed_packed))
        links.slot(feed_vectors)
        tall.cores()
        flat.cores()
        a = back(ready(), 0, widths, (), ())
        links.slot(a[3])
        tall.narrows()
        flat.acrosses()
        b = back(ready(), 1, widths, a[0], a[1])
        early = Reduction(links, *b[1])
        links.slot(b[3])
        flat.narrows()
        early.cores()
        c = back(ready(), 2, widths, b[0], ())
        links.slot(c[3])
        tall.acrosses()
        early.narrows()
        d = back(ready(), 3, widths, c[0], c[1])
        late = Reduction(links, *d[1])
        rows = place_pieces(
            rows_kernel,
            "vector_rows",
            place.astype(jnp.int32).reshape(1),
            (
                tuple(step[3] for step in (a, b, c, d)),
                tuple(step[4] for step in (a, b, c, d)),
                tuple(step[2] for step in (a, b, c, d)),
                feed_vectors,
                up_bias_grads,
                *norm,
            ),
            shaped((16, width), jnp.float32),
        )
        feeds = Ending(links, (tall, flat))
        earlies = Ending(links, (early,))
        lates = Ending(links, (late,))
        small = SmallSum(links, rows)
        top = crops // 2
        links.slot(d[3])
        feeds.alongs()
        early.acrosses()
        late.cores()
        upper = latents_step(ready(), d[0], 0, top, ())
        links.slot(upper)
        feeds.far_back()
        earlies.alongs()
        late.narrows()
        latents_gradient = latents_step(ready(), d[0], top, crops - top, (upper,))
        places = links.places()
        links.slot((latents_gradient, feeds.got, earlies.got))
        late.acrosses()
        feeds.near_back()
        earlies.far_back()
        small.step()
        links.slot((late.got, feeds.got, earlies.got, small.rows, places))
        lates.alongs()
        near_column, far_column = feeds.columns
        near_columns = feeds.across_back((near_column,))
        earlies.near_back()
        links.slot((lates.got, earlies.got, feeds.got))
        lates.along_back()
        far_columns = feeds.across_back((far_column,))
        early_columns = earlies.across_back((jnp.concatenate(earlies.columns, axis=0),))
        small.step()
        links.slot((lates.got, feeds.got, small.rows))
        late_columns = lates.across_back()
        feeds.core_back(
            tuple(column for pair in zip(near_columns, far_columns) for column in pair)
        )
        small.step()
        small.step()
        square = (
            shaped((width, units), jnp.float32),
            shaped((units, width), jnp.float32),
        )
        down_grad, out_grad, up_grad = place_pieces(
            finish_feed_kernel,
            "feed_places",
            places,
            (feeds.result,),
            (square[1], square[1], square[0]),
        )
        links.slot((lates.got, small.rows, up_grad))
        lates.core_back(late_columns)
        earlies.core_back(early_columns)
        small.step()
        rowwise = small.rows
        attend_matrix_grads = place_pieces(
            finish_kernel,
            "attend_places",
            places,
            ((earlies.result, lates.result),),
            (square[0],) * 3,
        )
    else:
        widths = (units, width - units)
        step = back(live, 0, widths, (), ())
        latents_gradient = latents_step(live, step[0], 0, crops, ())
        together = lambda own, rest: jnp.roll(
            jnp.concatenate([own, rest]).reshape(narrow, units), place, axis=0
        ).reshape(-1)
        shift_grad = step[4].sum(axis=0)
        rows = jnp.stack(
            [
                (step[3].sum(axis=1) - first_shift * shift_grad) / first_gain,
                shift_grad,
                *(feed_vectors[row] for row in range(4)),
                together(step[2][0][0], step[2][1][0]),
                together(step[2][0][2], step[2][1][2]),
                together(up_bias_grads[0][0], up_bias_grads[1][0]),
            ]
        )
        rowwise = lax.psum(rows, ("wide", "narrow"))
        joined = step[1][0]
        attend_matrix_grads = tuple(
            links.reduce_plain(
                joined[:, kind * units : (kind + 1) * units],
                lax.slice_in_dim(
                    joined,
                    3 * units + kind * widths[1],
                    3 * units + (kind + 1) * widths[1],
                    axis=1,
                ),
                1,
            )
            for kind in range(3)
        )
        down_grad, out_grad, up_grad = (
            links.reduce_plain(*grads, axis) for grads, axis in zip(feed_packed, (0, 0, 1))
        )
    own = lax.dynamic_slice_in_dim(rowwise[6:9], place * units, units, 1)
    return (
        block_output,
        latents_gradient,
        *attend_matrix_grads,
        out_grad,
        up_grad,
        down_grad,
        own[0],
        own[1],
        own[2],
        rowwise[4],
        rowwise[5],
        rowwise[0],
        rowwise[1],
        rowwise[2],
        rowwise[3],
    )


def solution(mesh):
    rows = P(("wide", "narrow"), None)
    columns = P(None, "narrow")
    units = P("narrow", None)
    vector = P("narrow")
    whole = P()
    return jax.shard_map(
        on_device,
        mesh=mesh,
        in_specs=(
            rows,
            rows,
            whole,
            whole,
            columns,
            columns,
            columns,
            units,
            columns,
            units,
            vector,
            vector,
            vector,
            whole,
            whole,
            whole,
            whole,
            whole,
            whole,
        ),
        out_specs=(
            rows,
            rows,
            columns,
            columns,
            columns,
            units,
            columns,
            units,
            vector,
            vector,
            vector,
            whole,
            whole,
            whole,
            whole,
            whole,
            whole,
        ),
        check_vma=False,
    )
```

```python
from functools import partial
import math

import jax
import jax.numpy as jnp
from jax import lax
from jax.experimental import pallas as pl
from jax.experimental.pallas import tpu as pltpu
from jax.sharding import PartitionSpec as P

HS = 128
CROP = 512


EPSILON = 1e-05


def dot(left, right, left_dim, right_dim):
    return lax.dot_general(
        left,
        right,
        (((left_dim,), (right_dim,)), ((), ())),
        preferred_element_type=jnp.float32,
    )


def unit_rows(rows):
    center = rows - jnp.mean(rows, axis=-1, keepdims=True)
    inverse = lax.rsqrt(jnp.mean(center * center, axis=-1, keepdims=True) + EPSILON)
    return center * inverse, inverse


def unit_rows_back(scaled, unit, inverse):
    inner = scaled - jnp.mean(scaled, axis=-1, keepdims=True)
    return (inner - unit * jnp.mean(scaled * unit, axis=-1, keepdims=True)) * inverse


def low(array):
    return array.astype(jnp.bfloat16)


def attend_kernel(first, start, carried, live_ref, source_ref, *refs):
    if first:
        gain_ref, shift_ref, *refs = refs
    query_weight, key_weight, value_weight, query_bias, value_bias, *refs = refs
    refs = refs[carried:]
    if first:
        normed_ref, *refs = refs
    query_ref, keys_ref, values_ref, weights_ref, attended_ref, inverse_ref = refs

    @pl.when(pl.program_id(0) + start < live_ref[0])
    def _():
        if first:
            unit, _ = unit_rows(source_ref[...].astype(jnp.float32))
            normed_ref[...] = low(unit * gain_ref[...] + shift_ref[...])
            normed = normed_ref[...]
        else:
            normed = source_ref[...]
        query_ref[...] = low(dot(normed, query_weight[...], 1, 0) + query_bias[...])
        keys_ref[...] = low(dot(normed, key_weight[...], 1, 0))
        values_ref[...] = low(dot(normed, value_weight[...], 1, 0) + value_bias[...])
        ones = jnp.ones((CROP, HS), jnp.bfloat16)
        for head in range(query_ref.shape[1] // HS):
            columns = pl.ds(head * HS, HS)
            scores = dot(query_ref[:, columns], keys_ref[:, columns], 1, 1)
            highest = jnp.max(scores, axis=-1, keepdims=True)
            weights = low(jnp.exp2((scores - highest) * (math.log2(math.e) / math.sqrt(HS))))
            weights_ref[head] = weights
            extended = jnp.concatenate([values_ref[:, columns], ones], axis=1)
            mixed = dot(weights, extended, 1, 0)
            inverse = 1.0 / mixed[:, HS:]
            inverse_ref[:, columns] = inverse
            attended_ref[:, columns] = low(mixed[:, :HS] * inverse)


def cut_kernel(places_ref, cuts, extra, *outputs):
    for pieces, target in zip(cuts, outputs):
        row = 0
        width = target.shape[1]
        for piece in pieces:
            rows = piece.shape[0]
            for side in range(piece.shape[1] // width):
                target[row : row + rows, :] = piece[:, side * width : (side + 1) * width]
                row += rows
    if extra:
        rows = [array[...].astype(jnp.float32).reshape(1, -1) for array in extra]
        rows += [jnp.zeros_like(rows[0])] * (EXTRA - len(rows))
        outputs[0][outputs[0].shape[0] - EXTRA :] = low(jnp.concatenate(rows, axis=0))


def fill_kernel(firsts, places_ref, near, far, *outputs):
    for pieces, core in ((near, places_ref[0]), (far, 1 - places_ref[0])):
        starts = (places_ref[1], 1 - places_ref[1], 1)
        for source, start, eighths, row in zip(pieces, starts, (1, 1, 2), firsts):
            width = source.shape[1]
            for output in outputs:
                size = output.shape[0] * eighths // 8
                base = core * (output.shape[0] // 2) + start * size
                rows = pl.ds(pl.multiple_of(base, size), size)
                for side in range(output.shape[1] // width):
                    output[rows, side * width : (side + 1) * width] = source[row : row + size, :]
                    row += size


EXTRA = 16


def gelu_pair(before):
    lower = 0.5 + 0.5 * lax.erf(before * math.sqrt(0.5))
    density = jnp.exp2(before * before * (-0.5 * math.log2(math.e)))
    slope = lower + before * density * (1.0 / math.sqrt(2.0 * math.pi))
    return before * lower, slope


def feed_kernel(
    crops,
    split,
    live_ref,
    latents_ref,
    cotangent_ref,
    attended_refs,
    out_weights,
    up_weights,
    down_weights,
    up_biases,
    out_bias,
    down_bias,
    gain,
    shift,
    output_ref,
    hidden_grad_ref,
    attended_grads,
    packed,
    up_bias_grads,
    vectors_ref,
    out_sums,
    up_sums,
    down_sums,
):
    step = pl.program_id(0)

    @pl.when(step == 0)
    def _():
        for sums in (*out_sums, *up_sums, *down_sums, *up_bias_grads, vectors_ref):
            sums[...] = jnp.zeros_like(sums)

    @pl.when(step >= live_ref[0])
    def _():
        output_ref[...] = jnp.zeros_like(output_ref)
        hidden_grad_ref[...] = jnp.zeros_like(hidden_grad_ref)

    @pl.when(step < live_ref[0])
    def _():
        hidden = latents_ref[...].astype(jnp.float32) + out_bias[...]
        for part in range(2):
            hidden = hidden + dot(attended_refs[part][...], out_weights[part][...], 1, 0)
        unit, inverse = unit_rows(hidden)
        normed = low(unit * gain[...] + shift[...])
        top = cotangent_ref[...]
        result = hidden + down_bias[...]
        second_grad = jnp.zeros(hidden.shape, jnp.float32)
        for part in range(2):
            before = dot(normed, up_weights[part][...], 1, 0) + up_biases[part][...]
            value, slope = gelu_pair(before)
            activated = low(value)
            result = result + dot(activated, down_weights[part][...], 1, 0)
            down_sums[part][...] += dot(activated, top, 0, 0)
            activated_grad = dot(top, down_weights[part][...], 1, 1)
            before_grad = low(activated_grad * slope)
            up_bias_grads[part][...] += jnp.sum(
                before_grad.astype(jnp.float32), axis=0, keepdims=True
            )
            up_sums[part][...] += dot(normed, before_grad, 0, 0)
            second_grad = second_grad + dot(before_grad, up_weights[part][...], 1, 1)
        output_ref[...] = low(result)
        top_grad = top.astype(jnp.float32)
        hidden_grad = top_grad + unit_rows_back(second_grad * gain[...], unit, inverse)
        hidden_grad_ref[...] = hidden_grad
        hidden_low = low(hidden_grad)
        for part in range(2):
            out_sums[part][...] += dot(attended_refs[part][...], hidden_low, 0, 0)
            attended_grads[part][...] = low(dot(hidden_low, out_weights[part][...], 1, 1))
        for row, term in enumerate((second_grad * unit, second_grad, hidden_grad, top_grad)):
            vectors_ref[row : row + 1] += jnp.sum(term, axis=0, keepdims=True)

    @pl.when(step == crops - 1)
    def _():
        if not split:
            for grads, sums in zip(packed, (down_sums, out_sums, up_sums)):
                for part in range(2):
                    grads[part][...] = low(sums[part][...])
            return
        for group, core in zip(packed, (live_ref[1], 1 - live_ref[1])):
            tall_ref, flat_ref = group
            rows = flat_ref.shape[0] // 2
            short = tall_ref.shape[0] // (4 * PIECES)
            half = tall_ref.shape[1] // 2
            for part in range(2):
                flat_ref[part * rows : (part + 1) * rows] = low(
                    up_sums[part][pl.ds(pl.multiple_of(core * rows, rows), rows), :]
                )
                for piece in range(PIECES):
                    start = core * (PIECES * short) + piece * short
                    source = pl.ds(pl.multiple_of(start, short), short)
                    for side in range(2):
                        base = part * rows + (2 * piece + side) * short
                        across = pl.ds(side * half, half)
                        for index, sums in enumerate((down_sums, out_sums)):
                            tall_ref[base : base + short, index * half : (index + 1) * half] = low(
                                sums[part][source, across]
                            )


def attend_back_kernel(
    crops,
    split,
    live_ref,
    normed_ref,
    queries,
    keys,
    values,
    weights,
    inverses,
    attended,
    attended_grads,
    matrices,
    previous,
    packed_before,
    grads,
    packed,
    bias_grads,
    gain_terms,
    shift_terms,
    joined,
    sums,
):
    step = pl.program_id(0)
    scale = 1.0 / math.sqrt(HS)
    widths = [ref.shape[1] for ref in queries]
    bases = (0, 3 * widths[0])

    @pl.when(step == 0)
    def _():
        sums[...] = jnp.zeros_like(sums)
        for part in range(2):
            bias_grads[part][...] = jnp.zeros_like(bias_grads[part])

    @pl.when(step < live_ref[0])
    def _():
        for part in range(2):
            for head in range(widths[part] // HS):
                columns = pl.ds(head * HS, HS)

                def put(kind, value):
                    value = low(value)
                    grads[kind][part][:, columns] = value
                    joined[:, pl.ds(bases[part] + kind * widths[part] + head * HS, HS)] = value

                inner = attended_grads[part][:, columns].astype(jnp.float32)
                inner = inner * inverses[part][:, columns]
                upstream = low(inner)
                total = jnp.sum(
                    inner * attended[part][:, columns].astype(jnp.float32), axis=1, keepdims=True
                )
                head_weights = weights[part][head]
                put(2, dot(head_weights, upstream, 0, 0))
                probs_grad = dot(upstream, values[part][:, columns], 1, 1)
                scores_grad = low(head_weights.astype(jnp.float32) * (probs_grad - total))
                put(0, dot(scores_grad, keys[part][:, columns], 1, 0) * scale)
                put(1, dot(scores_grad, queries[part][:, columns], 0, 0) * scale)
            for kind in range(3):
                bias_grads[part][kind : kind + 1] += jnp.sum(
                    grads[kind][part][...].astype(jnp.float32), axis=0, keepdims=True
                )
        sums[...] += dot(normed_ref[...], joined[...], 0, 0)

    @pl.when(step == crops - 1)
    def _():
        gain_terms[...] = jnp.zeros_like(gain_terms)
        shift_terms[...] = jnp.zeros_like(shift_terms)
        for part in range(2):
            for kind in range(3):
                matrix = matrices[kind][part]
                base = bases[part] + kind * widths[part]
                for start in range(0, widths[part], HS):
                    gain_terms[...] += sums[:, pl.ds(base + start, HS)] * matrix[
                        :, pl.ds(start, HS)
                    ].astype(jnp.float32)
                bias = bias_grads[part][kind : kind + 1]
                rough = low(bias)
                fine = low(bias - rough.astype(jnp.float32))
                shift_terms[...] += dot(
                    jnp.concatenate([rough, fine] + [jnp.zeros_like(rough)] * 6, axis=0),
                    matrix[...],
                    1,
                    1,
                )
        if not split:
            packed[0][...] = low(sums[...])
            return
        half = sums.shape[0] // 2
        for target, core in zip(packed, (live_ref[1], 1 - live_ref[1])):
            rows = pl.ds(pl.multiple_of(core * half, half), half)
            for part in range(2):
                target[part * half : (part + 1) * half] = low(
                    sums[rows, pl.ds(bases[part], 3 * widths[part])]
                )


def latents_kernel(
    first, live_ref, latents_ref, hidden_grad_ref, grads, matrices, gain_ref, previous, output_ref
):
    crop = pl.program_id(0) + first

    @pl.when(crop >= live_ref[0])
    def _():
        output_ref[...] = jnp.zeros_like(output_ref)

    @pl.when(crop < live_ref[0])
    def _():
        unit, inverse = unit_rows(latents_ref[...].astype(jnp.float32))
        upstream = jnp.zeros(output_ref.shape, jnp.float32)
        for kind in range(3):
            for grad, matrix in zip(grads[kind], matrices[kind]):
                upstream = upstream + dot(grad[...], matrix[...], 1, 1)
        output_ref[...] = hidden_grad_ref[...] + unit_rows_back(
            upstream * gain_ref[...], unit, inverse
        )


def finish_kernel(places_ref, groups, *outputs):
    def put(group):
        for index, source in enumerate(group):
            pieces = 16 // len(group)
            size = source.shape[0] // pieces
            width = source.shape[1] // 6
            for piece in range(pieces):
                start = pl.multiple_of(places_ref[index * pieces + piece] * size, size)
                for column in range(6):
                    phase, kind = column // 3, column % 3
                    outputs[kind][pl.ds(start, size), pl.ds(phase * width, width)] = source[
                        piece * size : (piece + 1) * size, pl.ds(column * width, width)
                    ].astype(jnp.float32)

    for half, group in enumerate(groups):
        pl.when(pl.program_id(0) == half)(partial(put, group))


def finish_feed_kernel(places_ref, sources, down_ref, out_ref, up_ref):
    half = up_ref.shape[1]
    for index, source in enumerate(sources):
        pieces = 16 // len(sources)
        size = source.shape[0] // pieces
        short = size // 2
        for piece in range(pieces):
            place = places_ref[index * pieces + piece]
            up_ref[pl.ds(pl.multiple_of(place * size, size), size), :] = source[
                piece * size : (piece + 1) * size, pl.ds(2 * half, half)
            ].astype(jnp.float32)
            rows = pl.ds(pl.multiple_of(place * short, short), short)
            for side in range(2):
                start = piece * size + side * short
                for column, target in enumerate((down_ref, out_ref)):
                    target[rows, pl.ds(side * half, half)] = source[
                        start : start + short, pl.ds(column * half, half)
                    ].astype(jnp.float32)


def rows_kernel(
    place_ref, gains, shifts, biases, feed_vectors, up_biases, gain_ref, shift_ref, rows_ref
):
    gain_terms = gains[0][...]
    shift_terms = shifts[0][...]
    for more in gains[1:]:
        gain_terms = gain_terms + more[...]
    for more in shifts[1:]:
        shift_terms = shift_terms + more[...]
    shift_grad = jnp.sum(shift_terms, axis=0, keepdims=True)
    unscaled = jnp.sum(gain_terms.T, axis=0, keepdims=True)
    rows_ref[...] = jnp.zeros_like(rows_ref)
    rows_ref[0:1] = (unscaled - shift_ref[...] * shift_grad) / gain_ref[...]
    rows_ref[1:2] = shift_grad
    rows_ref[2:6] = feed_vectors[0:4]

    def put(row, own, rest):
        own = jnp.concatenate(own, axis=1)
        rest = jnp.concatenate(rest, axis=1)
        rows_ref[row : row + 1] = jnp.where(
            place_ref[0] == 0,
            jnp.concatenate([own, rest], axis=1),
            jnp.concatenate([rest, own], axis=1),
        )

    for row, kind in ((6, 0), (7, 2)):
        put(row, *([pair[part][kind : kind + 1] for pair in biases] for part in range(2)))
    put(8, *([array[...]] for array in up_biases))


PIECES = 8
VMEM_LIMIT = 66_000_000
COST_SCALE = 8


def row_block(width, column=0):
    return pl.BlockSpec((CROP, width), lambda i, live: (i, column))


def fixed(rows, width, column=0):
    return pl.BlockSpec((rows, width), lambda i, live: (0, column), pipeline_mode=pl.Buffered(1))


def shaped(shape, dtype=jnp.bfloat16):
    return jax.ShapeDtypeStruct(shape, dtype)


def run(
    kernel, name, crops, in_specs, out_specs, out_shape, flops, moved, scratch=(), aliases=None
):
    return pl.pallas_call(
        kernel,
        input_output_aliases=aliases or {},
        name=name,
        out_shape=out_shape,
        grid_spec=pltpu.PrefetchScalarGridSpec(
            num_scalar_prefetch=1,
            grid=(crops,),
            in_specs=in_specs,
            out_specs=out_specs,
            scratch_shapes=scratch,
        ),
        compiler_params=pltpu.CompilerParams(
            dimension_semantics=("arbitrary",), vmem_limit_bytes=VMEM_LIMIT
        ),
        cost_estimate=pl.CostEstimate(
            flops=COST_SCALE * flops, bytes_accessed=COST_SCALE * moved, transcendentals=0
        ),
    )


def attend(live, source, norm, matrices, biases, start, size, previous=()):
    count, width = source.shape
    crops = count // CROP
    units = matrices[0].shape[1]
    heads = units // HS
    first = norm is not None
    vector = fixed(1, units)
    block = lambda width: pl.BlockSpec((CROP, width), lambda i, live: (i + start, 0))
    outs = (block(width),) * first + (
        block(units),
        block(units),
        block(units),
        pl.BlockSpec((None, heads, CROP, CROP), lambda i, live: (i + start, 0, 0, 0)),
        block(units),
        block(units),
    )
    rows = shaped((count, units))
    shapes = (shaped((count, width)),) * first + (
        rows,
        rows,
        rows,
        shaped((crops, heads, CROP, CROP)),
        rows,
        shaped((count, units), jnp.float32),
    )
    operands = (live, source, *(norm or ()), *matrices, *biases)
    done = size * CROP
    return run(
        partial(attend_kernel, first, start, len(previous)),
        "attend_first" if first else "attend_rest",
        size,
        (block(width),)
        + (fixed(1, width),) * (2 * first)
        + (fixed(width, units),) * 3
        + (vector,) * 2
        + (pl.BlockSpec(memory_space=pl.ANY),) * len(previous),
        outs,
        shapes,
        2 * done * units * (3 * width + 2 * CROP),
        done * (units * (12 + 2 * CROP // HS) + 4 * width),
        (),
        {len(operands) + i: i for i in range(len(previous))},
    )(*operands, *previous)


def feed(live, latents, cotangent, attended, outs, ups, downs, up_biases, vectors, split):
    count, width = latents.shape
    crops = count // CROP
    units = [array.shape[1] for array in attended]
    both = lambda make: tuple(make(size) for size in units)
    row_in = both(row_block)
    tall = both(lambda size: fixed(size, width))
    flat = both(lambda size: fixed(width, size))
    thin = both(lambda size: fixed(1, size))
    vector = fixed(1, width)
    sums = lambda dtype: (
        both(lambda size: dtype((size, width))),
        both(lambda size: dtype((width, size))),
        both(lambda size: dtype((size, width))),
    )
    if split:
        packed_specs = ((fixed(width, width), fixed(width, width // 2)),) * 2
        packed_shapes = ((shaped((width, width)), shaped((width, width // 2))),) * 2
    else:
        packed_specs = (tall, tall, flat)
        out_shapes, up_shapes, down_shapes = sums(shaped)
        packed_shapes = (down_shapes, out_shapes, up_shapes)
    return run(
        partial(feed_kernel, crops, split),
        "feed",
        crops,
        (row_block(width), row_block(width), row_in, tall, flat, tall, thin)
        + (vector,) * 4,
        (row_block(width), row_block(width), row_in, packed_specs, thin, fixed(8, width)),
        (
            shaped((count, width)),
            shaped((count, width), jnp.float32),
            both(lambda size: shaped((count, size))),
            packed_shapes,
            both(lambda size: shaped((1, size), jnp.float32)),
            shaped((8, width), jnp.float32),
        ),
        2 * count * width * width * 9,
        count * width * 14,
        sums(lambda shape: pltpu.VMEM(shape, jnp.float32)),
    )(live, latents, cotangent, attended, outs, ups, downs, up_biases, *vectors)


def attend_back(
    live, normed, saved, attended_grads, matrices, widths, phase, previous, packed_before, split
):
    count, width = normed.shape
    crops = count // CROP
    both = lambda make: tuple(make(size) for size in widths)
    units = [array.shape[1] for array in saved[0]]
    rows = both(lambda size: row_block(size, phase))
    heads = both(
        lambda size: pl.BlockSpec(
            (None, size // HS, CROP, CROP), lambda i, live: (i, phase, 0, 0)
        )
    )
    flat = both(lambda size: fixed(width, size, phase))
    queries, keys, values, weights, attended, inverses = saved
    joined = 3 * sum(widths)
    if split:
        packed_specs = (fixed(width, joined // 2, phase % 2),) * 2
        packed_shapes = (shaped((width, joined)),) * 2
    else:
        packed_specs = (fixed(width, joined),)
        packed_shapes = (shaped((width, joined)),)
    operands = (
        live,
        normed,
        queries,
        keys,
        values,
        weights,
        inverses,
        attended,
        attended_grads,
        matrices,
    )
    before = len(jax.tree.leaves(operands))
    carried = len(jax.tree.leaves(previous))
    aliases = {before + i: i for i in range(carried)}
    for i in range(len(packed_before)):
        aliases[before + carried + i] = 6 + i
    untouched = lambda arrays: jax.tree.map(lambda _: pl.BlockSpec(memory_space=pl.ANY), arrays)
    return run(
        partial(attend_back_kernel, crops, split),
        "attend_back",
        crops,
        (row_block(width), rows, rows, rows, heads, rows, rows, rows, (flat,) * 3)
        + (untouched(previous), untouched(packed_before)),
        (
            (rows,) * 3,
            packed_specs,
            both(lambda size: fixed(8, size)),
            fixed(width, HS),
            fixed(8, width),
        ),
        (
            (tuple(shaped((count, size)) for size in units),) * 3,
            packed_shapes,
            both(lambda size: shaped((8, size), jnp.float32)),
            shaped((width, HS), jnp.float32),
            shaped((8, width), jnp.float32),
        ),
        2 * count * sum(widths) * (3 * width + 4 * CROP),
        count * (sum(widths) * (18 + 2 * CROP // HS) + 2 * width),
        (
            pltpu.VMEM((CROP, joined), jnp.bfloat16),
            pltpu.VMEM((width, joined), jnp.float32),
        ),
        aliases,
    )(*operands, previous, packed_before)


def latents_back(live, latents, hidden_grad, grads, matrices, gain, first, crops, previous):
    count, width = latents.shape
    block = lambda size: pl.BlockSpec((CROP, size), lambda i, live: (i + first, 0))
    rows = tuple(tuple(block(array.shape[1]) for array in kind) for kind in grads)
    flat = tuple(tuple(fixed(*array.shape) for array in kind) for kind in matrices)
    operands = (live, latents, hidden_grad, grads, matrices, gain)
    before = len(jax.tree.leaves(operands))
    return run(
        partial(latents_kernel, first),
        "latents_back",
        crops,
        (block(width), block(width), rows, flat, fixed(1, width))
        + (tuple(pl.BlockSpec(memory_space=pl.ANY) for _ in previous),),
        block(width),
        shaped((count, width), jnp.float32),
        2 * crops * CROP * width * width * 3,
        crops * CROP * width * 16,
        (),
        {before + i: i for i in range(len(previous))},
    )(*operands, previous)


def place_pieces(kernel, name, places, operands, out_shape, parts=1):
    return pl.pallas_call(
        kernel,
        name=name,
        out_shape=out_shape,
        grid_spec=pltpu.PrefetchScalarGridSpec(
            num_scalar_prefetch=1,
            grid=(parts,),
            in_specs=jax.tree.map(
                lambda array: pl.BlockSpec(array.shape, lambda i, places: (0, 0)), operands
            ),
            out_specs=jax.tree.map(
                lambda array: pl.BlockSpec(
                    (array.shape[0], array.shape[1] // parts), lambda i, places: (0, i)
                ),
                out_shape,
            ),
        ),
        compiler_params=pltpu.CompilerParams(
            dimension_semantics=("arbitrary",), vmem_limit_bytes=VMEM_LIMIT
        ),
    )(places, *operands)


def cut_weights(places, weights, cuts, extra=()):
    width = min(weight.shape[1] for weight in weights)
    eighth = lambda i, places: (places[0] * 4 + places[1], 0)
    quarter = lambda i, places: (places[0] * 2 + 1, 0)
    specs = tuple(
        tuple(
            pl.BlockSpec(
                (weights[k].shape[0] // (8 if shared else 4), weights[k].shape[1]),
                eighth if shared else quarter,
            )
            for k, shared in cut
        )
        for cut in cuts
    )
    rows = [sum(weights[k].size // (8 if shared else 4) for k, shared in cut) // width for cut in cuts]
    if extra:
        rows[0] += EXTRA
    shapes = tuple(shaped((count, width)) for count in rows)
    whole = lambda array: pl.BlockSpec(array.shape, lambda i, places: (0,) * len(array.shape))
    return pl.pallas_call(
        cut_kernel,
        name="cut_weights",
        out_shape=shapes,
        grid_spec=pltpu.PrefetchScalarGridSpec(
            num_scalar_prefetch=1,
            grid=(1,),
            in_specs=(specs, tuple(whole(array) for array in extra)),
            out_specs=tuple(whole(shape) for shape in shapes),
        ),
        compiler_params=pltpu.CompilerParams(
            dimension_semantics=("arbitrary",), vmem_limit_bytes=VMEM_LIMIT
        ),
    )(places, tuple(tuple(weights[k] for k, _ in cut) for cut in cuts), extra)


def pair_perm(size, bit):
    return [(i, i ^ bit) for i in range(size)]


def after(value, *needed):
    return lax.optimization_barrier((value, needed))[0]


class Links:
    def __init__(self):
        self.wide = lax.axis_size("wide")
        self.narrow = lax.axis_size("narrow")
        self.paired = self.narrow == 2 and self.wide == 16
        self.index = lax.axis_index("wide")
        self.core = self.index % 2
        self.across = (self.index // 2) % 2
        self.along = self.index // 4
        self.token = ()
        self.sent = ()

    def slot(self, token):
        self.token = token
        self.sent = ()

    def swap(self, array, bit):
        return lax.ppermute(array, "wide", pair_perm(self.wide, bit))

    def swap_narrow(self, array):
        return lax.ppermute(array, "narrow", [(0, 1), (1, 0)])

    def others(self, weight, axis):
        whole = lax.all_gather(weight, "narrow", axis=0, tiled=False)
        whole = jnp.roll(whole, -lax.axis_index("narrow"), axis=0)[1:]
        return jnp.concatenate([whole[i] for i in range(self.narrow - 1)], axis=axis)

    def places(self):
        return jnp.stack(
            [
                (self.core ^ core) * 8 + (self.across ^ across) * 4 + (self.along ^ along)
                for core in range(2)
                for across in range(2)
                for along in (0, 2, 1, 3)
            ]
        ).astype(jnp.int32)

    def reduce_plain(self, own, other, axis):
        width = own.shape[axis]
        parts = jnp.stack(
            [own]
            + [
                lax.slice_in_dim(other, i * width, (i + 1) * width, axis=axis)
                for i in range(self.narrow - 1)
            ]
        )
        parts = jnp.roll(parts, lax.axis_index("narrow"), axis=0)
        mine = lax.psum_scatter(parts, "narrow", scatter_dimension=0, tiled=True)[0]
        return lax.psum(mine, "wide").astype(jnp.float32)


def total(terms, size):
    parts = [
        lax.dynamic_slice_in_dim(array, start, size, 0).astype(jnp.float32)
        for array, start in terms
    ]
    return sum(parts[1:], parts[0]).astype(jnp.bfloat16)


def moved(terms, rows):
    return [(array, start + rows) for array, start in terms]


class Exchange:
    def __init__(self, links):
        self.links = links

    def waiting(self, terms):
        return [(after(array, self.links.token), start) for array, start in terms]

    def exchange(self, arrays, *sends):
        arrays = tuple(after(array, self.links.token) for array in arrays)
        self.links.sent += arrays
        return tuple(send(array) for send, array in zip(sends, arrays))


class Reduction(Exchange):
    def __init__(self, links, keep, give):
        super().__init__(links)
        self.rows = keep.shape[0] // 2
        self.own = [(keep, 0)]
        self.other = [(keep, self.rows)]
        self.give = give

    def cores(self):
        (got,) = self.exchange([self.give], lambda array: self.links.swap(array, 1))
        self.own += [(got, 0)]
        self.other += [(got, self.rows)]

    def narrows(self):
        give = total(self.waiting(self.other), self.rows)
        (got,) = self.exchange([give], self.links.swap_narrow)
        self.own += [(got, 0)]
        self.other = []
        self.got = got

    def acrosses(self):
        size = self.rows // 2
        across = self.links.across
        parts = [self.waiting(terms) for terms in (self.own, self.other) if terms]
        gives = [total(moved(terms, (1 - across) * size), size) for terms in parts]
        give = jnp.concatenate(gives, axis=0) if len(gives) > 1 else gives[0]
        (got,) = self.exchange([give], lambda array: self.links.swap(array, 2))
        self.own = moved(self.own, across * size) + [(got, 0)]
        if self.other:
            self.other = moved(self.other, across * size) + [(got, size)]
        self.rows = size
        self.got = got


class Ending(Exchange):
    def __init__(self, links, groups):
        super().__init__(links)
        self.groups = groups
        self.swaps = [
            lambda array: links.swap(array, 4),
            lambda array: links.swap(array, 8),
            lambda array: links.swap(array, 12),
        ]

    def alongs(self):
        size = self.groups[0].rows // 4
        for group in self.groups:
            group.own = self.waiting(group.own)
        terms = lambda group, bit: moved(group.own, (self.links.along ^ bit) * size)
        gives = [
            jnp.concatenate([total(terms(group, bit), size) for group in self.groups], axis=1)
            for bit in range(1, 4)
        ]
        got = self.exchange(gives, *self.swaps)
        self.parts = [terms(group, 0) for group in self.groups]
        self.size = size
        self.got = got

    def piece(self):
        got = [after(array, self.links.token) for array in self.got]
        pieces = []
        column = 0
        for terms in self.parts:
            width = terms[0][0].shape[1]
            mine = [
                (lax.slice_in_dim(array, column, column + width, axis=1), 0) for array in got
            ]
            pieces.append(total(self.waiting(terms) + mine, self.size))
            column += width
        return jnp.concatenate(pieces, axis=1)

    def along_back(self):
        piece = self.piece()
        self.got = self.exchange([piece] * 3, *self.swaps)
        near, far, opposite = self.got
        self.column = (piece, far, near, opposite)

    def far_back(self):
        piece = self.piece()
        self.got = self.exchange([piece], self.swaps[1])
        self.column = (piece, *self.got)

    def near_back(self):
        column = self.whole_column()
        self.got = self.exchange([column], self.swaps[0])
        self.columns = (column, *self.got)

    def whole_column(self):
        return jnp.concatenate([after(array, self.links.token) for array in self.column], axis=0)

    def across_back(self, columns=None):
        columns = columns or (self.whole_column(),)
        self.got = self.exchange(columns, *(len(columns) * (lambda array: self.links.swap(array, 2),)))
        return (*columns, *self.got)

    def core_back(self, columns):
        swap = lambda array: self.links.swap(array, 1)
        got = self.exchange(columns, *(len(columns) * (swap,)))
        self.result = (*columns, *got)


class SmallSum(Exchange):
    def __init__(self, links, rows):
        super().__init__(links)
        self.rows = rows
        self.left = [
            lambda rows: links.swap(rows, 2),
            lambda rows: links.swap(rows, 1),
            links.swap_narrow,
            lambda rows: links.swap(rows, 4),
            lambda rows: links.swap(rows, 8),
        ]

    def step(self):
        (got,) = self.exchange([self.rows], self.left.pop(0))
        self.rows = self.rows + got


def on_device(
    latents,
    cotangent,
    crop_counts,
    image_device,
    query_weight,
    key_weight,
    value_weight,
    out_weight,
    up_weight,
    down_weight,
    query_bias,
    value_bias,
    up_bias,
    out_bias,
    down_bias,
    first_gain,
    first_shift,
    second_gain,
    second_shift,
):
    links = Links()
    paired = links.paired
    count = latents.shape[0]
    crops = count // CROP
    width = latents.shape[1]
    narrow = links.narrow
    place = lax.axis_index("narrow")
    owned = jnp.sum(jnp.where(image_device == lax.axis_index("wide"), crop_counts, 0))
    live = jnp.stack([owned - place * crops, links.core]).astype(jnp.int32)
    units = query_weight.shape[1]
    vector = lambda array: array.reshape(1, -1)
    own_biases = jnp.stack([query_bias, value_bias, up_bias])
    rows_of = lambda array: tuple(array[i : i + 1].astype(jnp.float32) for i in range(3))
    norm = (vector(first_gain), vector(first_shift))
    own_weights = (query_weight, key_weight, value_weight)
    feed_weights = (out_weight, down_weight, up_weight)
    first_step = lambda live, start, size, previous: attend(
        live, latents, norm, own_weights, rows_of(own_biases)[:2], start, size, previous
    )
    rest_step = lambda live: attend(
        live, first, None, rest_weights, rows_of(rest_biases)[:2], 0, crops
    )
    if paired:
        spots = jnp.stack([links.core, links.across]).astype(jnp.int32)
        unfilled = lambda weights: tuple(shaped(weight.shape) for weight in weights)
        cores = lambda pieces: tuple(links.swap(piece, 1) for piece in pieces)
        begin = crops // 2
        part = lambda numbers, shared: tuple((k, shared) for k in numbers)
        cuts = cut_weights(
            spots,
            own_weights + feed_weights,
            (part(range(3), True), part(range(3), False) + part(range(3, 6), True)),
            (query_bias, value_bias, up_bias),
        )
        shared, direct = (links.swap_narrow(cut) for cut in cuts)
        early = first_step(after(live, cuts), 0, begin, ())
        shared = after(shared, early[0])
        (feed_cut,) = cut_weights(
            after(spots, early[0]), feed_weights, (part(range(3), False),)
        )
        first, *saved_own = first_step(
            after(live, (shared, feed_cut)), begin, crops - begin, tuple(early)
        )
        feed_direct = links.swap_narrow(feed_cut)
        relayed = links.swap(shared, 2)
        rest_biases = shared[shared.shape[0] - EXTRA :]
        pieces = after((shared, relayed, direct), (first, feed_cut))
        far = cores(pieces)
        rest_weights = place_pieces(
            partial(fill_kernel, (0, 0, 0)),
            "fill_attend",
            spots,
            (pieces, far),
            unfilled(own_weights),
        )
        rows = sum(weight.shape[0] // 4 for weight in own_weights)
        feed_shared = pieces[2][rows:]
        feed_relayed = links.swap(feed_shared, 2)
        saved_rest = rest_step(after(live, feed_shared))
        later = after((feed_relayed, feed_direct), saved_rest[0])
        later_far = cores(later)
        rest_out, rest_down, rest_up = place_pieces(
            partial(fill_kernel, (rows, 0, 0)),
            "fill_feed",
            spots,
            ((pieces[2], *later), (far[2], *later_far)),
            unfilled(feed_weights),
        )
    else:
        first, *saved_own = first_step(live, 0, crops, ())
        rest_biases = lax.all_gather(own_biases, "narrow", axis=0)
        rest_biases = jnp.roll(rest_biases, -place, axis=0).transpose(1, 0, 2).reshape(3, -1)
        rest_biases = rest_biases[:, units:]
        rest_weights = tuple(links.others(weight, 1) for weight in own_weights)
        saved_rest = rest_step(live)
        rest_out = links.others(out_weight, 0)
        rest_up = links.others(up_weight, 1)
        rest_down = links.others(down_weight, 0)
    up_biases = (rows_of(own_biases)[2], rows_of(rest_biases)[2])
    matrices = tuple(zip(own_weights, rest_weights))
    outs = (out_weight, rest_out)
    ups = (up_weight, rest_up)
    downs = (down_weight, rest_down)
    saved = tuple(zip(saved_own, saved_rest))
    (
        block_output,
        hidden_grad,
        attended_grads,
        feed_packed,
        up_bias_grads,
        feed_vectors,
    ) = feed(
        live,
        latents,
        cotangent,
        saved[4],
        outs,
        ups,
        downs,
        up_biases,
        [vector(array) for array in (out_bias, down_bias, second_gain, second_shift)],
        paired,
    )

    def back(live, phase, widths, previous, packed_before):
        return attend_back(
            live,
            first,
            saved,
            attended_grads,
            matrices,
            widths,
            phase,
            previous,
            packed_before,
            paired,
        )

    def latents_step(live, grads, start, size, previous):
        return latents_back(
            live, latents, hidden_grad, grads, matrices, norm[0], start, size, previous
        )

    if paired:
        phases = units // HS
        widths = (HS, (width - units) // phases)
        ready = lambda: after(live, links.sent)
        tall, flat = (Reduction(links, keep, give) for keep, give in zip(*feed_packed))
        links.slot(feed_vectors)
        tall.cores()
        flat.cores()
        a = back(ready(), 0, widths, (), ())
        links.slot(a[3])
        tall.narrows()
        flat.acrosses()
        b = back(ready(), 1, widths, a[0], a[1])
        early = Reduction(links, *b[1])
        links.slot(b[3])
        flat.narrows()
        early.cores()
        c = back(ready(), 2, widths, b[0], ())
        links.slot(c[3])
        tall.acrosses()
        early.narrows()
        d = back(ready(), 3, widths, c[0], c[1])
        late = Reduction(links, *d[1])
        rows = place_pieces(
            rows_kernel,
            "vector_rows",
            place.astype(jnp.int32).reshape(1),
            (
                tuple(step[3] for step in (a, b, c, d)),
                tuple(step[4] for step in (a, b, c, d)),
                tuple(step[2] for step in (a, b, c, d)),
                feed_vectors,
                up_bias_grads,
                *norm,
            ),
            shaped((16, width), jnp.float32),
        )
        feeds = Ending(links, (tall, flat))
        earlies = Ending(links, (early,))
        lates = Ending(links, (late,))
        small = SmallSum(links, rows)
        top = crops // 2
        links.slot(d[3])
        feeds.alongs()
        early.acrosses()
        late.cores()
        upper = latents_step(ready(), d[0], 0, top, ())
        links.slot(upper)
        feeds.far_back()
        earlies.alongs()
        late.narrows()
        latents_gradient = latents_step(ready(), d[0], top, crops - top, (upper,))
        places = links.places()
        links.slot((latents_gradient, feeds.got, earlies.got))
        late.acrosses()
        feeds.near_back()
        earlies.far_back()
        small.step()
        links.slot((late.got, feeds.got, earlies.got, small.rows, places))
        lates.alongs()
        near_column, far_column = feeds.columns
        near_columns = feeds.across_back((near_column,))
        earlies.near_back()
        links.slot((lates.got, earlies.got, feeds.got))
        lates.along_back()
        far_columns = feeds.across_back((far_column,))
        early_columns = earlies.across_back((jnp.concatenate(earlies.columns, axis=0),))
        small.step()
        links.slot((lates.got, feeds.got, small.rows))
        late_columns = lates.across_back()
        feeds.core_back(
            tuple(column for pair in zip(near_columns, far_columns) for column in pair)
        )
        small.step()
        square = (
            shaped((width, units), jnp.float32),
            shaped((units, width), jnp.float32),
        )
        down_grad, out_grad, up_grad = place_pieces(
            finish_feed_kernel,
            "feed_places",
            places,
            (feeds.result,),
            (square[1], square[1], square[0]),
        )
        links.slot((lates.got, small.rows, up_grad))
        lates.core_back(late_columns)
        earlies.core_back(early_columns)
        small.step()
        small.step()
        rowwise = small.rows
        attend_matrix_grads = place_pieces(
            finish_kernel,
            "attend_places",
            places,
            ((earlies.result, lates.result),),
            (square[0],) * 3,
            2,
        )
    else:
        widths = (units, width - units)
        step = back(live, 0, widths, (), ())
        latents_gradient = latents_step(live, step[0], 0, crops, ())
        together = lambda own, rest: jnp.roll(
            jnp.concatenate([own, rest]).reshape(narrow, units), place, axis=0
        ).reshape(-1)
        shift_grad = step[4].sum(axis=0)
        rows = jnp.stack(
            [
                (step[3].sum(axis=1) - first_shift * shift_grad) / first_gain,
                shift_grad,
                *(feed_vectors[row] for row in range(4)),
                together(step[2][0][0], step[2][1][0]),
                together(step[2][0][2], step[2][1][2]),
                together(up_bias_grads[0][0], up_bias_grads[1][0]),
            ]
        )
        rowwise = lax.psum(rows, ("wide", "narrow"))
        joined = step[1][0]
        attend_matrix_grads = tuple(
            links.reduce_plain(
                joined[:, kind * units : (kind + 1) * units],
                lax.slice_in_dim(
                    joined,
                    3 * units + kind * widths[1],
                    3 * units + (kind + 1) * widths[1],
                    axis=1,
                ),
                1,
            )
            for kind in range(3)
        )
        down_grad, out_grad, up_grad = (
            links.reduce_plain(*grads, axis) for grads, axis in zip(feed_packed, (0, 0, 1))
        )
    own = lax.dynamic_slice_in_dim(rowwise[6:9], place * units, units, 1)
    return (
        block_output,
        latents_gradient,
        *attend_matrix_grads,
        out_grad,
        up_grad,
        down_grad,
        own[0],
        own[1],
        own[2],
        rowwise[4],
        rowwise[5],
        rowwise[0],
        rowwise[1],
        rowwise[2],
        rowwise[3],
    )


def solution(mesh):
    rows = P(("wide", "narrow"), None)
    columns = P(None, "narrow")
    units = P("narrow", None)
    vector = P("narrow")
    whole = P()
    return jax.shard_map(
        on_device,
        mesh=mesh,
        in_specs=(
            rows,
            rows,
            whole,
            whole,
            columns,
            columns,
            columns,
            units,
            columns,
            units,
            vector,
            vector,
            vector,
            whole,
            whole,
            whole,
            whole,
            whole,
            whole,
        ),
        out_specs=(
            rows,
            rows,
            columns,
            columns,
            columns,
            units,
            columns,
            units,
            vector,
            vector,
            vector,
            whole,
            whole,
            whole,
            whole,
            whole,
            whole,
        ),
        check_vma=False,
    )
```
